256 devices in a mesh: expert: 32 (over y, x, core), dp: 8 (over z).
Axes of the slice: x: 4, y: 4, z: 8, core: 2. Of those that a mesh axis runs over, the one named last changes fastest.
Arguments:
- tokens: bfloat16 [32768, 2048], P(('expert', 'dp')), may hold values from -6 to 6
- cotangent: bfloat16 [32768, 2048], P(('expert', 'dp')), may hold values from -6 to 6
- routes: int32 [32768, 4], P(('expert', 'dp')), may hold values from 0 to 31, all different within a row; in each aligned block of 128 rows (0 to 127, 128 to 255, ...) at most 24 rows name the same one
- gate_values: bfloat16 [32768, 4], P(('expert', 'dp')), may hold values from 0.099609375 to 1
- w_gate: bfloat16 [32, 2048, 512], P('expert', 'dp'), may hold values from -0.125 to 0.125
- w_up: bfloat16 [32, 2048, 512], P('expert', 'dp'), may hold values from -0.125 to 0.125
- w_down: bfloat16 [32, 512, 2048], P('expert', None, 'dp'), may hold values from -0.25 to 0.25
Outputs:
- token_grad: bfloat16 [32768, 2048], P(('expert', 'dp'))
- gate_weight_grad: bfloat16 [32, 2048, 512], P('expert', 'dp')
- up_weight_grad: bfloat16 [32, 2048, 512], P('expert', 'dp')
- down_weight_grad: bfloat16 [32, 512, 2048], P('expert', None, 'dp')
The draws below stay inside these ranges and needn't reach their ends.
Inputs may be any that keep to these rules, and one draw needn't show every extreme that they name: `routes`: each row names 4 different experts. Among the rows of one device no expert is named more than 24 times, and some device names some expert exactly 24 times.
All inputs are finite; a program needn't handle non-finite values.
Results may differ from the reference program's by a relative error of at most 0.017.
Values may be sent and summed in bfloat16 or wider, within the bound.
No kernel may reach another device: no remote copies, remote signals or barrier semaphores. Data moves between devices by JAX's collectives and lax.ppermute only.
A program may use at most 128 MiB of HBM per device.

```python
import math
import jax
import jax.numpy as jnp
import numpy as np
from jax import lax

D = 2048
FF = 512
TOP = 4
TOK_DEV = 128
EXPERTS = 32
CAP = 24
TOKENS = 32768
N_EXPERT = 32
N_DP = 8


def block_scale(key, dims, pieces, low, top_value):
    level, own = 1.0, jax.random.fold_in(key, 6)
    for dim, blocks in pieces:
        steps = jnp.exp(jax.random.uniform(jax.random.fold_in(own, dim), (blocks,), jnp.float32, low / len(pieces), top_value / len(pieces)))
        level = level * jnp.repeat(steps, dims[dim] // blocks).reshape([-1 if axis == dim else 1 for axis in range(len(dims))])
    return level


def assign_block(stream_key, own, number, rows, number_of, top, most, skew):
    sequence = jax.random.permutation(stream_key, number_of)
    crowded, ordinary = load_shares(number_of, rows * top, most, skew, True), load_shares(number_of, rows * top, most, skew, False)
    places = jnp.arange(number_of)

    def named(lengths, turn):
        used = int((lengths > 0).sum())
        fixed = max(1, used // 4)
        passed = fixed + (places - fixed + turn * (used - fixed)) % max(1, number_of - fixed)
        return jnp.zeros((number_of,), jnp.int32).at[sequence[jnp.where(places < fixed, places, passed)]].set(jnp.asarray(lengths, jnp.int32))

    lengths = jnp.where(number % 4 == 0, named(crowded, number // 4), named(ordinary, number - number // 4 - 1))
    mixed = jax.random.permutation(jax.random.fold_in(own, 3), number_of)
    source_of, taker = mixed[0:number_of // 2 * 2:2], mixed[1:number_of // 2 * 2:2]
    room = jnp.minimum(lengths[source_of] - 1, most - lengths[taker]) // 2
    room = jnp.where((source_of == sequence[0]) | (taker == sequence[0]) | (lengths[taker] == 0), 0, jnp.maximum(room, 0))
    passed = jax.random.randint(jax.random.fold_in(own, 4), (number_of // 2,), 0, 1 << 20) % (room + 1)
    lengths = lengths.at[source_of].add(-passed).at[taker].add(passed)
    items = jnp.searchsorted(jnp.cumsum(lengths), jnp.arange(rows * top), side="right").astype(jnp.int32)
    table = items.reshape(top, rows).T
    table = table[jax.random.permutation(jax.random.fold_in(own, 1), rows)]
    turn = jax.random.randint(jax.random.fold_in(own, 2), (rows, 1), 0, top)
    return jnp.take_along_axis(table, (jnp.arange(top)[None, :] + turn) % top, axis=1)


def load_shares(amount, total, most, skew, full):
    loads = [(1 << 20) // math.isqrt(rank ** skew) + 1 for rank in range(1, amount + 1)]
    largest = most if full else min(most, max(-(-total // amount), total * loads[0] // sum(loads)))
    least = 1 if total - largest >= amount - 1 else 0
    holding, rest = [largest] + [least] * (amount - 1), total - largest - least * (amount - 1)
    while rest > 0:
        free = [i for i in range(1, amount) if holding[i] < largest] or [i for i in range(1, amount) if holding[i] < most]
        pool, left = sum([loads[i] for i in free]), rest
        for i in free:
            addition = min(most - holding[i], max(1, left * loads[i] // pool), rest)
            holding[i] = holding[i] + addition
            rest = rest - addition
    return np.array(holding)


def gaussian(key, extent, spread, bound, shards=(), kind=jnp.bfloat16):
    values = jax.random.normal(key, extent, jnp.float32) * spread
    if len(shards) > 0:
        values = block_scale(key, extent, shards, -0.22, 0.18) * values
    return jnp.clip(values, min=-bound, max=bound).astype(kind)


def setup_inputs(seed: int = 0) -> dict:
    splits = jax.random.split(jax.random.key(seed), 8)
    tokens = gaussian(splits[0], (TOKENS, D), 1.0, 6.0, ((0, 256),))
    cotangent = gaussian(splits[1], (TOKENS, D), 1.0, 6.0, ((0, 256),))
    routes_keys = jax.random.split(jax.random.fold_in(splits[2], 1), TOKENS // TOK_DEV)
    routes_turns = jax.random.permutation(jax.random.fold_in(splits[2], 3), TOKENS // TOK_DEV)
    routes = jax.vmap(lambda own, number: assign_block(jax.random.fold_in(splits[2], 2), own, number, TOK_DEV, EXPERTS, TOP, CAP, 2))(routes_keys, routes_turns).reshape((TOKENS, TOP))
    gate_values = jnp.clip(jnp.exp(math.log(1.0) - 2.306499 * jax.random.uniform(splits[3], (TOKENS, TOP), jnp.float32) ** block_scale(splits[3], (TOKENS, TOP), ((0, 256),), -0.2, 0.2)), 0.099609375, 1.0).astype(jnp.bfloat16)
    w_gate = gaussian(splits[4], (EXPERTS, D, FF), D ** -0.5, 0.125, ((0, 32), (1, 8)))
    w_up = gaussian(splits[5], (EXPERTS, D, FF), D ** -0.5, 0.125, ((0, 32), (1, 8)))
    w_down = gaussian(splits[6], (EXPERTS, FF, D), FF ** -0.5, 0.25, ((0, 32), (2, 8)))
    return {"tokens": tokens, "cotangent": cotangent, "routes": routes, "gate_values": gate_values, "w_gate": w_gate, "w_up": w_up, "w_down": w_down}


def expert_pass(x_rows, dy_rows, gate_rows, weight_gate, weight_up, weight_down):
    gate_pre = jnp.dot(x_rows, weight_gate, preferred_element_type=jnp.float32)
    up_pre = jnp.dot(x_rows, weight_up, preferred_element_type=jnp.float32)
    sigmoid_gate = 1.0 / (1.0 + jnp.exp(-gate_pre))
    activated = gate_pre * sigmoid_gate
    hidden = (activated * up_pre).astype(jnp.bfloat16)
    scaled = (gate_rows[:, None].astype(jnp.float32) * dy_rows.astype(jnp.float32)).astype(jnp.bfloat16)
    hidden_grad = lax.dot_general(scaled, weight_down, (((1,), (1,)), ((), ())), preferred_element_type=jnp.float32)
    gate_grad = (hidden_grad * up_pre * sigmoid_gate * (1.0 + gate_pre * (1.0 - sigmoid_gate))).astype(jnp.bfloat16)
    up_grad = (hidden_grad * activated).astype(jnp.bfloat16)
    row_grad = lax.dot_general(gate_grad, weight_gate, (((1,), (1,)), ((), ())), preferred_element_type=jnp.float32)
    row_grad = row_grad + lax.dot_general(up_grad, weight_up, (((1,), (1,)), ((), ())), preferred_element_type=jnp.float32)
    return hidden, scaled, gate_grad, up_grad, row_grad.astype(jnp.bfloat16)


def group_sum(left, right):
    left_groups = left.reshape(N_DP, -1, left.shape[1]).astype(jnp.float32)
    right_groups = right.reshape(N_DP, -1, right.shape[1]).astype(jnp.float32)
    partial_sums = jnp.einsum("prd,prf->pdf", left_groups, right_groups)
    rounded = lax.optimization_barrier(partial_sums.astype(jnp.bfloat16))
    return jnp.sum(rounded.astype(jnp.float32), axis=0).astype(jnp.bfloat16)


def reference(tokens, cotangent, routes, gate_values, w_gate, w_up, w_down):
    blocks = N_EXPERT * N_DP
    per_expert = N_DP * N_EXPERT * CAP
    expert_ids = routes.reshape(blocks, TOK_DEV * TOP).astype(jnp.int32)
    onehot = (expert_ids[:, :, None] == jnp.arange(EXPERTS, dtype=jnp.int32)[None, None, :]).astype(jnp.int32)
    before = jnp.cumsum(onehot, axis=1) - onehot
    slot = jnp.sum(before * onehot, axis=2).astype(jnp.int32)
    block_ids = jnp.arange(blocks, dtype=jnp.int32)[:, None]
    source_dev = block_ids // N_DP
    group_ids = block_ids % N_DP
    position = (group_ids * N_EXPERT + source_dev) * CAP + slot
    flat_dest = (expert_ids * per_expert + position).reshape(-1).astype(jnp.int32)
    assigns = TOKENS * TOP
    row_index = jnp.full((EXPERTS * per_expert,), assigns, jnp.int32).at[flat_dest].set(jnp.arange(assigns, dtype=jnp.int32))
    tokens_pad = jnp.concatenate([tokens, jnp.zeros((1, D), tokens.dtype)], axis=0)
    cot_pad = jnp.concatenate([cotangent, jnp.zeros((1, D), cotangent.dtype)], axis=0)
    gate_pad = jnp.concatenate([gate_values.reshape(-1), jnp.zeros((1,), gate_values.dtype)], axis=0)

    def one_expert(inputs):
        indices, weight_gate, weight_up, weight_down = inputs
        token_ids = (indices // TOP).astype(jnp.int32)
        x_rows = tokens_pad[token_ids]
        dy_rows = cot_pad[token_ids]
        gate_rows = gate_pad[indices]
        hidden, scaled, gate_grad, up_grad, row_grad = expert_pass(x_rows, dy_rows, gate_rows, weight_gate, weight_up, weight_down)
        return group_sum(x_rows, gate_grad), group_sum(x_rows, up_grad), group_sum(hidden, scaled), row_grad

    grad_gate, grad_up, grad_down, row_grads = lax.map(one_expert, (row_index.reshape(EXPERTS, per_expert), w_gate, w_up, w_down))
    all_rows = row_grads.reshape(EXPERTS * per_expert, D)
    dest_table = flat_dest.reshape(TOKENS, TOP)
    summed = jnp.zeros((TOKENS, D), jnp.float32)
    for which in range(TOP):
        summed = summed + all_rows[dest_table[:, which]].astype(jnp.float32)
    return summed.astype(jnp.bfloat16), grad_gate, grad_up, grad_down
```

```python
import jax
import jax.numpy as jnp
from jax import lax
from jax.experimental.layout import Layout, with_layout_constraint
from jax.sharding import PartitionSpec as P


def slot_masks(routes, gate_values, experts, capacity):
    tok_dev = routes.shape[0]
    ids = jnp.arange(experts, dtype=jnp.int32)
    hit = routes[:, :, None] == ids[None, None, :]
    member = jnp.any(hit, axis=1)
    gate = jnp.sum(
        jnp.where(hit, gate_values.astype(jnp.float32)[:, :, None], 0.0), axis=1
    )
    row = lax.broadcasted_iota(jnp.int32, (tok_dev, tok_dev), 0)
    col = lax.broadcasted_iota(jnp.int32, (tok_dev, tok_dev), 1)
    earlier = (row < col).astype(jnp.bfloat16)
    before = lax.dot_general(
        member.astype(jnp.bfloat16),
        earlier,
        (((0,), (0,)), ((), ())),
        preferred_element_type=jnp.float32,
    ).astype(jnp.int32)
    rank = jnp.where(member.T, before, -1)
    place = rank[:, None, :] == jnp.arange(capacity, dtype=jnp.int32)[None, :, None]
    place = place.reshape(experts * capacity, tok_dev)
    weight = jnp.broadcast_to(gate.T[:, None, :], (experts, capacity, tok_dev)).reshape(
        experts * capacity, tok_dev
    )
    return place.astype(jnp.bfloat16), jnp.where(place, weight, 0.0).astype(jnp.bfloat16)


def row_major(a):
    return with_layout_constraint(a, Layout(major_to_minor=(0, 1)))


def matmul(a, b, dims):
    return lax.dot_general(a, b, (dims, ((), ())), preferred_element_type=jnp.float32)


def local(tokens, cotangent, routes, gate_values, w_gate, w_up, w_down):
    experts = lax.axis_size("expert")
    tok_dev, model_width = tokens.shape
    fan_out = routes.shape[1]
    hidden_width = w_gate.shape[2]
    capacity = min(tok_dev, 3 * tok_dev * fan_out // (2 * experts))

    shard = jnp.concatenate([w_gate[0], w_up[0], w_down[0].T], axis=1)
    full = row_major(lax.all_gather(row_major(shard), "dp", axis=0, tiled=True))

    place, weighted = slot_masks(routes, gate_values, experts, capacity)

    def exchange(rows):
        return lax.all_to_all(
            rows.reshape(experts, capacity, model_width),
            "expert",
            split_axis=0,
            concat_axis=0,
            tiled=True,
        ).reshape(experts * capacity, model_width)

    x_rows = exchange(matmul(place, tokens, ((1,), (0,))).astype(jnp.bfloat16))
    scaled = exchange(matmul(weighted, cotangent, ((1,), (0,))).astype(jnp.bfloat16))

    pre = matmul(x_rows, full[:, : 2 * hidden_width], ((1,), (0,)))
    gate_pre = pre[:, :hidden_width]
    up_pre = pre[:, hidden_width:]
    sigmoid_gate = 1.0 / (1.0 + jnp.exp(-gate_pre))
    activated = gate_pre * sigmoid_gate
    hidden = (activated * up_pre).astype(jnp.bfloat16)
    hidden_grad = matmul(scaled, full[:, 2 * hidden_width :], ((1,), (0,)))
    gate_grad = (
        hidden_grad * up_pre * sigmoid_gate * (1.0 + gate_pre * (1.0 - sigmoid_gate))
    ).astype(jnp.bfloat16)
    up_grad = (hidden_grad * activated).astype(jnp.bfloat16)
    both_grad = jnp.concatenate([gate_grad, up_grad], axis=1)

    in_term = matmul(x_rows, both_grad, ((0,), (0,))).astype(jnp.bfloat16)
    down_term = matmul(scaled, hidden, ((0,), (0,))).astype(jnp.bfloat16)
    terms = jnp.concatenate([in_term, down_term], axis=1)
    sums = row_major(lax.psum_scatter(row_major(terms), "dp", scatter_dimension=0, tiled=True))

    row_grad = matmul(both_grad, full[:, : 2 * hidden_width], ((1,), (1,)))
    returned = exchange(row_grad.astype(jnp.bfloat16))
    token_grad = matmul(place, returned, ((0,), (0,))).astype(jnp.bfloat16)
    return (
        token_grad,
        sums[None, :, :hidden_width],
        sums[None, :, hidden_width : 2 * hidden_width],
        sums[:, 2 * hidden_width :].T[None],
    )


def solution(mesh):
    in_specs = (
        P(("expert", "dp"), None),
        P(("expert", "dp"), None),
        P(("expert", "dp"), None),
        P(("expert", "dp"), None),
        P("expert", "dp", None),
        P("expert", "dp", None),
        P("expert", None, "dp"),
    )
    out_specs = (
        P(("expert", "dp"), None),
        P("expert", "dp", None),
        P("expert", "dp", None),
        P("expert", None, "dp"),
    )
    return jax.shard_map(local, mesh=mesh, in_specs=in_specs, out_specs=out_specs, check_vma=False)
```

```python
import jax
import jax.numpy as jnp
from jax import lax
from jax.experimental import pallas as pl
from jax.experimental.pallas import tpu as pltpu
from jax.sharding import PartitionSpec as P

ROWS = 256
COLS = 256


def matmul(a, b, dims=((1,), (0,))):
    return lax.dot_general(a, b, (dims, ((), ())), preferred_element_type=jnp.float32)


def pack_kernel(capacity, routes_ref, gate_ref, tokens_ref, cotangent_ref, packed_ref, rank_ref):
    some, tok_dev = rank_ref.shape
    fan_out = routes_ref.shape[0]
    width = tokens_ref.shape[1]
    ids = lax.broadcasted_iota(jnp.int32, (some, tok_dev), 0) + pl.program_id(0) * some
    member = jnp.zeros((some, tok_dev), jnp.float32)
    gate = jnp.zeros((some, tok_dev), jnp.float32)
    for k in range(fan_out):
        hit = routes_ref[k : k + 1, :] == ids
        member = jnp.where(hit, 1.0, member)
        gate = jnp.where(hit, gate_ref[k : k + 1, :], gate)
    row = lax.broadcasted_iota(jnp.int32, (tok_dev, tok_dev), 0)
    col = lax.broadcasted_iota(jnp.int32, (tok_dev, tok_dev), 1)
    before = matmul(member.astype(jnp.bfloat16), (row < col).astype(jnp.bfloat16))
    rank = jnp.where(member > 0.5, before, -1.0)
    rank_ref[...] = rank.astype(jnp.int32)
    slots = lax.broadcasted_iota(jnp.int32, (capacity, tok_dev), 0).astype(jnp.float32)
    place, weighted = [], []
    for e in range(some):
        here = jnp.broadcast_to(rank[e : e + 1, :], (capacity, tok_dev)) == slots
        place.append(jnp.where(here, 1.0, 0.0))
        weighted.append(
            jnp.where(here, jnp.broadcast_to(gate[e : e + 1, :], (capacity, tok_dev)), 0.0)
        )
    place = jnp.concatenate(place, axis=0).astype(jnp.bfloat16)
    weighted = jnp.concatenate(weighted, axis=0).astype(jnp.bfloat16)
    packed_ref[:, :width] = matmul(place, tokens_ref[...]).astype(packed_ref.dtype)
    packed_ref[:, width:] = matmul(weighted, cotangent_ref[...]).astype(packed_ref.dtype)


def pack(routes, gate_values, tokens, cotangent, experts, capacity):
    tok_dev, width = tokens.shape
    fan_out = routes.shape[1]
    some = 8

    def whole(*shape):
        return pl.BlockSpec(shape, lambda i: (0, 0))

    return pl.pallas_call(
        lambda *refs: pack_kernel(capacity, *refs),
        grid=(experts // some,),
        in_specs=[
            whole(fan_out, tok_dev),
            whole(fan_out, tok_dev),
            whole(tok_dev, width),
            whole(tok_dev, width),
        ],
        out_specs=[
            pl.BlockSpec((some * capacity, 2 * width), lambda i: (i, 0)),
            pl.BlockSpec((some, tok_dev), lambda i: (i, 0)),
        ],
        out_shape=[
            jax.ShapeDtypeStruct((experts * capacity, 2 * width), tokens.dtype),
            jax.ShapeDtypeStruct((experts, tok_dev), jnp.int32),
        ],
        compiler_params=pltpu.CompilerParams(vmem_limit_bytes=60 << 20),
        cost_estimate=pl.CostEstimate(
            flops=4 * experts * capacity * tok_dev * width,
            bytes_accessed=4 * experts * capacity * width,
            transcendentals=0,
        ),
        name="pack",
    )(routes.T, gate_values.T.astype(jnp.float32), tokens, cotangent)


def stack_kernel(gate_ref, up_ref, down_ref, rank_ref, out_ref):
    out_ref[0] = gate_ref[0]
    out_ref[1] = up_ref[0]
    out_ref[2] = down_ref[0].T


def stack(w_gate, w_up, w_down, rank):
    _, rows, width = w_gate.shape
    return pl.pallas_call(
        stack_kernel,
        in_specs=[pl.BlockSpec(memory_space=pltpu.VMEM)] * 3 + [pl.BlockSpec(memory_space=pl.ANY)],
        out_specs=pl.BlockSpec(memory_space=pltpu.VMEM),
        out_shape=jax.ShapeDtypeStruct((3, rows, width), w_gate.dtype),
        compiler_params=pltpu.CompilerParams(vmem_limit_bytes=60 << 20),
        name="stack",
    )(w_gate, w_up, w_down, rank)


def terms_kernel(row_steps, rows_ref, x_ref, scaled_ref, w_ref, grads_ref, terms_ref, grads, hidden_t):
    i = pl.program_id(0)
    width = w_ref.shape[1]
    ff = w_ref.shape[2]

    @pl.when(i < row_steps)
    def _():
        x = rows_ref[:, :width]
        gate_pre = matmul(x, w_ref[0])
        up_pre = matmul(x, w_ref[1])
        hidden_grad = matmul(rows_ref[:, width:], w_ref[2])
        sig = 1.0 / (1.0 + jnp.exp(-gate_pre))
        activated = gate_pre * sig
        hidden = activated * up_pre
        gate_grad = hidden_grad * up_pre * sig * (1.0 + gate_pre * (1.0 - sig))
        up_grad = hidden_grad * activated
        start = pl.multiple_of(i * ROWS, ROWS)
        both = jnp.concatenate(
            [gate_grad.astype(jnp.bfloat16), up_grad.astype(jnp.bfloat16)], axis=1
        )
        grads[pl.ds(start, ROWS), :] = both
        grads_ref[...] = both
        hidden_t[:, pl.ds(start, ROWS)] = hidden.astype(jnp.bfloat16).T

    @pl.when(i >= row_steps)
    def _():
        both = matmul(x_ref[...], grads[...], ((0,), (0,))).astype(jnp.bfloat16)
        terms_ref[0] = both[:, :ff]
        terms_ref[1] = both[:, ff:]
        down = matmul(hidden_t[...], scaled_ref[...]).astype(jnp.bfloat16)
        terms_ref[2] = jnp.concatenate([down[: ff // 2], down[ff // 2 :]], axis=1)


def terms_of(received, full):
    rows, width2 = received.shape
    _, width, ff = full.shape
    row_steps, col_steps = rows // ROWS, width // COLS

    def col(i):
        return jnp.maximum(i - row_steps, 0)

    def row(i):
        return jnp.minimum(i, row_steps - 1)

    return pl.pallas_call(
        lambda *refs: terms_kernel(row_steps, *refs),
        grid=(row_steps + col_steps,),
        in_specs=[
            pl.BlockSpec((ROWS, width2), lambda i: (row(i), 0)),
            pl.BlockSpec((rows, COLS), lambda i: (0, col(i))),
            pl.BlockSpec((rows, COLS), lambda i: (0, col_steps + col(i))),
            pl.BlockSpec((3, width, ff), lambda i: (0, 0, 0), pipeline_mode=pl.Buffered(1)),
        ],
        out_specs=[
            pl.BlockSpec((ROWS, 2 * ff), lambda i: (row(i), 0)),
            pl.BlockSpec((3, COLS, ff), lambda i: (0, col(i), 0)),
        ],
        out_shape=[
            jax.ShapeDtypeStruct((rows, 2 * ff), jnp.bfloat16),
            jax.ShapeDtypeStruct((3, width, ff), jnp.bfloat16),
        ],
        scratch_shapes=[
            pltpu.VMEM((rows, 2 * ff), jnp.bfloat16),
            pltpu.VMEM((ff, rows), jnp.bfloat16),
        ],
        compiler_params=pltpu.CompilerParams(vmem_limit_bytes=60 << 20),
        cost_estimate=pl.CostEstimate(
            flops=12 * rows * width * ff,
            bytes_accessed=2 * (4 * rows * width + 6 * width * ff),
            transcendentals=rows * ff,
        ),
        name="terms",
    )(received, received, received, full)


def split_kernel(sums_ref, gate_ref, up_ref, down_ref):
    gate_ref[0] = sums_ref[0]
    up_ref[0] = sums_ref[1]
    half = sums_ref.shape[1]
    down_ref[0, :half] = sums_ref[2, :, : COLS]
    down_ref[0, half:] = sums_ref[2, :, COLS :]


def split(sums):
    _, rows, ff = sums.shape
    vmem = pl.BlockSpec(memory_space=pltpu.VMEM)
    return pl.pallas_call(
        split_kernel,
        in_specs=[vmem],
        out_specs=[vmem] * 3,
        out_shape=[
            jax.ShapeDtypeStruct((1, rows, ff), sums.dtype),
            jax.ShapeDtypeStruct((1, rows, ff), sums.dtype),
            jax.ShapeDtypeStruct((1, ff, rows), sums.dtype),
        ],
        compiler_params=pltpu.CompilerParams(vmem_limit_bytes=60 << 20),
        name="split",
    )(sums)


def local(tokens, cotangent, routes, gate_values, w_gate, w_up, w_down):
    experts = lax.axis_size("expert")
    tok_dev, model_width = tokens.shape
    fan_out = routes.shape[1]
    capacity = min(tok_dev, 3 * tok_dev * fan_out // (2 * experts))

    def exchange(rows):
        return lax.all_to_all(
            rows.reshape(experts, capacity, rows.shape[1]),
            "expert",
            split_axis=0,
            concat_axis=0,
            tiled=True,
        ).reshape(rows.shape)

    packed, rank = pack(routes, gate_values, tokens, cotangent, experts, capacity)
    received = exchange(packed)
    full = lax.all_gather(stack(w_gate, w_up, w_down, rank), "dp", axis=1, tiled=True)

    both_grad, terms = terms_of(received, full)
    sums = lax.psum_scatter(terms, "dp", scatter_dimension=1, tiled=True)

    ff = w_gate.shape[2]
    row_grad = matmul(both_grad[:, :ff], full[0], ((1,), (1,))) + matmul(
        both_grad[:, ff:], full[1], ((1,), (1,))
    )
    returned = exchange(row_grad.astype(jnp.bfloat16))
    place = rank[:, None, :] == jnp.arange(capacity, dtype=jnp.int32)[None, :, None]
    place = place.reshape(experts * capacity, tok_dev).astype(jnp.bfloat16)
    token_grad = matmul(place, returned, ((0,), (0,))).astype(jnp.bfloat16)
    return (token_grad, *split(sums))


def solution(mesh):
    in_specs = (
        P(("expert", "dp"), None),
        P(("expert", "dp"), None),
        P(("expert", "dp"), None),
        P(("expert", "dp"), None),
        P("expert", "dp", None),
        P("expert", "dp", None),
        P("expert", None, "dp"),
    )
    out_specs = (
        P(("expert", "dp"), None),
        P("expert", "dp", None),
        P("expert", "dp", None),
        P("expert", None, "dp"),
    )
    return jax.shard_map(local, mesh=mesh, in_specs=in_specs, out_specs=out_specs, check_vma=False)
```

```python
import jax
import jax.numpy as jnp
from jax import lax
from jax.experimental import pallas as pl
from jax.experimental.pallas import tpu as pltpu
from jax.sharding import PartitionSpec as P

ROWS = 384
COLS = 256
TERM_COLS = 512
PACK_COLS = 512


def matmul(a, b, dims=((1,), (0,))):
    return lax.dot_general(a, b, (dims, ((), ())), preferred_element_type=jnp.float32)


def pack_kernel(
    capacity,
    routes_ref,
    gate_ref,
    tokens_hbm,
    cotangent_hbm,
    w_gate_hbm,
    w_up_hbm,
    w_down_hbm,
    packed_hbm,
    rank_ref,
    shard_hbm,
    tokens,
    shards,
    down,
    place,
    packed,
    in_sems,
    w_sems,
    shard_sems,
    out_sems,
):
    experts, tok_dev = rank_ref.shape
    width = tokens_hbm.shape[1]
    sources = [tokens_hbm, cotangent_hbm]
    row_copies = [
        pltpu.make_async_copy(sources[k], tokens.at[k], in_sems.at[k]) for k in range(2)
    ]
    w_copies = [
        pltpu.make_async_copy(w_gate_hbm.at[0], shards.at[0], w_sems.at[0]),
        pltpu.make_async_copy(w_up_hbm.at[0], shards.at[1], w_sems.at[1]),
        pltpu.make_async_copy(w_down_hbm.at[0], down, w_sems.at[2]),
    ]
    for copy in row_copies + w_copies:
        copy.start()

    ids = lax.broadcasted_iota(jnp.int32, (experts, tok_dev), 0)
    gates = gate_ref[...].astype(jnp.float32)
    member = jnp.zeros((experts, tok_dev), jnp.float32)
    gate = jnp.zeros((experts, tok_dev), jnp.float32)
    for k in range(routes_ref.shape[0]):
        hit = routes_ref[k : k + 1, :] == ids
        member = jnp.where(hit, 1.0, member)
        gate = jnp.where(hit, gates[k : k + 1, :], gate)
    row = lax.broadcasted_iota(jnp.int32, (tok_dev, tok_dev), 0)
    col = lax.broadcasted_iota(jnp.int32, (tok_dev, tok_dev), 1)
    before = matmul(member.astype(jnp.bfloat16), (row < col).astype(jnp.bfloat16))
    rank = jnp.where(member > 0.5, before, -1.0)
    rank_ref[...] = rank.astype(jnp.int32)
    slots = lax.broadcasted_iota(jnp.int32, (capacity, tok_dev), 0).astype(jnp.float32)
    for e in range(0, experts, 2):
        here, gate_here = [], []
        for f in (e, e + 1):
            mask = jnp.broadcast_to(rank[f : f + 1, :], (capacity, tok_dev)) == slots
            here.append(jnp.where(mask, 1.0, 0.0))
            gate_here.append(
                jnp.where(mask, jnp.broadcast_to(gate[f : f + 1, :], (capacity, tok_dev)), 0.0)
            )
        span = slice(e * capacity, (e + 2) * capacity)
        place[0, span, :] = jnp.concatenate(here, axis=0).astype(place.dtype)
        place[1, span, :] = jnp.concatenate(gate_here, axis=0).astype(place.dtype)

    shard_copies = [
        pltpu.make_async_copy(shards.at[k], shard_hbm.at[k], shard_sems.at[k]) for k in range(3)
    ]
    out_copies = []
    for k in range(2):
        row_copies[k].wait()
        for start in range(0, width, PACK_COLS):
            span = slice(k * width + start, k * width + start + PACK_COLS)
            packed[:, span] = matmul(
                place[k], tokens[k, :, start : start + PACK_COLS]
            ).astype(packed.dtype)
            cols = (slice(None), pl.ds(k * width + start, PACK_COLS))
            out_copies.append(
                pltpu.make_async_copy(
                    packed.at[cols], packed_hbm.at[cols], out_sems.at[len(out_copies)]
                )
            )
            out_copies[-1].start()
        if k == 0:
            w_copies[0].wait()
            shard_copies[0].start()
            w_copies[1].wait()
            shard_copies[1].start()
            w_copies[2].wait()
            shards[2] = down[...].T
            shard_copies[2].start()
    for copy in shard_copies + out_copies:
        copy.wait()


def pack(routes, gate_values, tokens, cotangent, w_gate, w_up, w_down, experts, capacity):
    tok_dev, width = tokens.shape
    slots = experts * capacity
    vmem = pl.BlockSpec(memory_space=pltpu.VMEM)
    hbm = pl.BlockSpec(memory_space=pl.ANY)
    return pl.pallas_call(
        lambda *refs: pack_kernel(capacity, *refs),
        in_specs=[vmem] * 2 + [hbm] * 5,
        out_specs=[hbm, vmem, hbm],
        out_shape=[
            jax.ShapeDtypeStruct((slots, 2 * width), tokens.dtype),
            jax.ShapeDtypeStruct((experts, tok_dev), jnp.int32),
            jax.ShapeDtypeStruct((3, *w_gate.shape[1:]), w_gate.dtype),
        ],
        scratch_shapes=[
            pltpu.VMEM((2, tok_dev, width), tokens.dtype),
            pltpu.VMEM((3, *w_gate.shape[1:]), w_gate.dtype),
            pltpu.VMEM(w_down.shape[1:], w_down.dtype),
            pltpu.VMEM((2, slots, tok_dev), jnp.bfloat16),
            pltpu.VMEM((slots, 2 * width), tokens.dtype),
            pltpu.SemaphoreType.DMA((2,)),
            pltpu.SemaphoreType.DMA((3,)),
            pltpu.SemaphoreType.DMA((3,)),
            pltpu.SemaphoreType.DMA((2 * width // PACK_COLS,)),
        ],
        compiler_params=pltpu.CompilerParams(vmem_limit_bytes=60 << 20),
        cost_estimate=pl.CostEstimate(
            flops=4 * slots * tok_dev * width,
            bytes_accessed=4 * slots * width,
            transcendentals=0,
        ),
        name="pack",
    )(routes.T, gate_values.T, tokens, cotangent, w_gate, w_up, w_down)


def terms_kernel(
    rows_hbm,
    w_hbm,
    grads_hbm,
    terms_hbm,
    rows,
    w,
    grads,
    hidden_t,
    terms,
    row_sems,
    w_sems,
    grads_sem,
    out_sems,
):
    _, width, ff = w_hbm.shape
    n = rows.shape[0]

    def row_copy(k, left, size):
        span = (pl.ds(k * ROWS, ROWS), pl.ds(left, size))
        return pltpu.make_async_copy(
            rows_hbm.at[span], rows.at[span], row_sems.at[k + (1 if left else 0) + (k > 0)]
        )

    x_copy = row_copy(0, 0, width)
    scaled_copy = row_copy(0, width, width)
    later = [row_copy(k, 0, 2 * width) for k in range(1, n // ROWS)]
    w_copies = [pltpu.make_async_copy(w_hbm.at[k], w.at[k], w_sems.at[k]) for k in range(3)]
    for copy in [x_copy, *w_copies[:2], scaled_copy, w_copies[2], *later]:
        copy.start()

    for k in range(n // ROWS):
        span = slice(k * ROWS, (k + 1) * ROWS)
        if k == 0:
            x_copy.wait()
            w_copies[0].wait()
        else:
            later[k - 1].wait()
        x = rows[span, :width]
        gate_pre = matmul(x, w[0])
        sig = 1.0 / (1.0 + jnp.exp(-gate_pre))
        activated = gate_pre * sig
        slope = sig * (1.0 + gate_pre * (1.0 - sig))
        if k == 0:
            w_copies[1].wait()
        up_pre = matmul(x, w[1])
        hidden_t[:, span] = (activated * up_pre).astype(jnp.bfloat16).T
        if k == 0:
            scaled_copy.wait()
            w_copies[2].wait()
        hidden_grad = matmul(rows[span, width:], w[2])
        grads[span, :ff] = (hidden_grad * up_pre * slope).astype(jnp.bfloat16)
        grads[span, ff:] = (hidden_grad * activated).astype(jnp.bfloat16)

    out_copies = [pltpu.make_async_copy(grads, grads_hbm, grads_sem)]
    out_copies[0].start()
    for k, start in enumerate(range(0, width, TERM_COLS)):
        span = slice(start, start + TERM_COLS)
        both = matmul(rows[:, span], grads[...], ((0,), (0,))).astype(jnp.bfloat16)
        terms[0, span, :] = both[:, :ff]
        terms[1, span, :] = both[:, ff:]
        down = matmul(hidden_t[...], rows[:, width + start : width + start + TERM_COLS])
        down = down.astype(jnp.bfloat16)
        for c in range(0, TERM_COLS, COLS):
            for h in range(0, ff, COLS):
                terms[2, start + c : start + c + COLS, h : h + COLS] = down[
                    h : h + COLS, c : c + COLS
                ]
        block = (slice(None), pl.ds(start, TERM_COLS), slice(None))
        out_copies.append(
            pltpu.make_async_copy(terms.at[block], terms_hbm.at[block], out_sems.at[k])
        )
        out_copies[-1].start()
    for copy in out_copies:
        copy.wait()


def terms_of(received, full):
    rows, width2 = received.shape
    _, width, ff = full.shape
    hbm = pl.BlockSpec(memory_space=pl.ANY)
    return pl.pallas_call(
        terms_kernel,
        in_specs=[hbm] * 2,
        out_specs=[hbm] * 2,
        out_shape=[
            jax.ShapeDtypeStruct((rows, 2 * ff), jnp.bfloat16),
            jax.ShapeDtypeStruct((3, width, ff), jnp.bfloat16),
        ],
        scratch_shapes=[
            pltpu.VMEM((rows, width2), jnp.bfloat16),
            pltpu.VMEM((3, width, ff), jnp.bfloat16),
            pltpu.VMEM((rows, 2 * ff), jnp.bfloat16),
            pltpu.VMEM((ff, rows), jnp.bfloat16),
            pltpu.VMEM((3, width, ff), jnp.bfloat16),
            pltpu.SemaphoreType.DMA((1 + rows // ROWS,)),
            pltpu.SemaphoreType.DMA((3,)),
            pltpu.SemaphoreType.DMA,
            pltpu.SemaphoreType.DMA((width // TERM_COLS,)),
        ],
        compiler_params=pltpu.CompilerParams(vmem_limit_bytes=60 << 20),
        cost_estimate=pl.CostEstimate(
            flops=12 * rows * width * ff,
            bytes_accessed=2 * (2 * rows * width + 6 * width * ff),
            transcendentals=rows * ff,
        ),
        name="terms",
    )(received, full)


def split_kernel(sums_ref, gate_ref, up_ref, down_ref, held, in_sems, out_sems):
    half = held.shape[1]
    arrive = [pltpu.make_async_copy(sums_ref.at[k], held.at[k], in_sems.at[k]) for k in range(3)]
    leave = [
        [pltpu.make_async_copy(held.at[0], gate_ref.at[0], out_sems.at[0])],
        [pltpu.make_async_copy(held.at[1], up_ref.at[0], out_sems.at[1])],
        [
            pltpu.make_async_copy(
                held.at[2, :, pl.ds(h * half, half)],
                down_ref.at[0, pl.ds(h * half, half), :],
                out_sems.at[2 + h],
            )
            for h in range(2)
        ],
    ]
    for copy in arrive:
        copy.start()
    for copy, copies in zip(arrive, leave):
        copy.wait()
        for c in copies:
            c.start()
    for copies in leave:
        for c in copies:
            c.wait()


def split(sums):
    _, rows, ff = sums.shape
    hbm = pl.BlockSpec(memory_space=pl.ANY)
    return pl.pallas_call(
        split_kernel,
        in_specs=[hbm],
        out_specs=[hbm] * 3,
        out_shape=[
            jax.ShapeDtypeStruct((1, rows, ff), sums.dtype),
            jax.ShapeDtypeStruct((1, rows, ff), sums.dtype),
            jax.ShapeDtypeStruct((1, ff, rows), sums.dtype),
        ],
        scratch_shapes=[
            pltpu.VMEM(sums.shape, sums.dtype),
            pltpu.SemaphoreType.DMA((3,)),
            pltpu.SemaphoreType.DMA((4,)),
        ],
        compiler_params=pltpu.CompilerParams(vmem_limit_bytes=60 << 20),
        name="split",
    )(sums)


def local(tokens, cotangent, routes, gate_values, w_gate, w_up, w_down):
    experts = lax.axis_size("expert")
    tok_dev, model_width = tokens.shape
    fan_out = routes.shape[1]
    capacity = min(tok_dev, 3 * tok_dev * fan_out // (2 * experts))

    def exchange(rows):
        return lax.all_to_all(
            rows.reshape(experts, capacity, rows.shape[1]),
            "expert",
            split_axis=0,
            concat_axis=0,
            tiled=True,
        ).reshape(rows.shape)

    packed, rank, shard = pack(
        routes, gate_values, tokens, cotangent, w_gate, w_up, w_down, experts, capacity
    )
    received = exchange(packed)
    full = lax.all_gather(shard, "dp", axis=1, tiled=True)

    both_grad, terms = terms_of(received, full)
    sums = lax.psum_scatter(terms, "dp", scatter_dimension=1, tiled=True)

    ff = w_gate.shape[2]
    row_grad = matmul(both_grad[:, :ff], full[0], ((1,), (1,))) + matmul(
        both_grad[:, ff:], full[1], ((1,), (1,))
    )
    returned = exchange(row_grad.astype(jnp.bfloat16))
    place = rank[:, None, :] == jnp.arange(capacity, dtype=jnp.int32)[None, :, None]
    place = place.reshape(experts * capacity, tok_dev).astype(jnp.bfloat16)
    token_grad = matmul(place, returned, ((0,), (0,))).astype(jnp.bfloat16)
    return (token_grad, *split(sums))


def solution(mesh):
    in_specs = (
        P(("expert", "dp"), None),
        P(("expert", "dp"), None),
        P(("expert", "dp"), None),
        P(("expert", "dp"), None),
        P("expert", "dp", None),
        P("expert", "dp", None),
        P("expert", None, "dp"),
    )
    out_specs = (
        P(("expert", "dp"), None),
        P("expert", "dp", None),
        P("expert", "dp", None),
        P("expert", None, "dp"),
    )
    return jax.shard_map(local, mesh=mesh, in_specs=in_specs, out_specs=out_specs, check_vma=False)
```

```python
import jax
import jax.numpy as jnp
from jax import lax
from jax.experimental import pallas as pl
from jax.experimental.pallas import tpu as pltpu
from jax.sharding import PartitionSpec as P

ROWS = 384
COLS = 256
TERM_COLS = 512
PACK_COLS = 512


def matmul(a, b, dims=((1,), (0,))):
    return lax.dot_general(a, b, (dims, ((), ())), preferred_element_type=jnp.float32)


def pack_kernel(
    capacity,
    routes_ref,
    gate_ref,
    tokens_hbm,
    cotangent_hbm,
    w_gate_hbm,
    w_up_hbm,
    w_down_hbm,
    packed_hbm,
    rank_ref,
    shard_a_hbm,
    shard_b_hbm,
    tokens,
    shards,
    down,
    place,
    packed,
    in_sems,
    w_sems,
    shard_sems,
    out_sems,
):
    experts, tok_dev = rank_ref.shape
    width = tokens_hbm.shape[1]
    sources = [tokens_hbm, cotangent_hbm]
    row_copies = [
        pltpu.make_async_copy(sources[k], tokens.at[k], in_sems.at[k]) for k in range(2)
    ]
    w_copies = [
        pltpu.make_async_copy(w_gate_hbm.at[0], shards.at[0], w_sems.at[0]),
        pltpu.make_async_copy(w_up_hbm.at[0], shards.at[1], w_sems.at[1]),
        pltpu.make_async_copy(w_down_hbm.at[0], down, w_sems.at[2]),
    ]
    for copy in row_copies + w_copies:
        copy.start()

    ids = lax.broadcasted_iota(jnp.int32, (experts, tok_dev), 0)
    gates = gate_ref[...].astype(jnp.float32)
    member = jnp.zeros((experts, tok_dev), jnp.float32)
    gate = jnp.zeros((experts, tok_dev), jnp.float32)
    for k in range(routes_ref.shape[0]):
        hit = routes_ref[k : k + 1, :] == ids
        member = jnp.where(hit, 1.0, member)
        gate = jnp.where(hit, gates[k : k + 1, :], gate)
    row = lax.broadcasted_iota(jnp.int32, (tok_dev, tok_dev), 0)
    col = lax.broadcasted_iota(jnp.int32, (tok_dev, tok_dev), 1)
    before = matmul(member.astype(jnp.bfloat16), (row < col).astype(jnp.bfloat16))
    rank = jnp.where(member > 0.5, before, -1.0)
    rank_ref[...] = rank.astype(jnp.int32)
    slots = lax.broadcasted_iota(jnp.int32, (capacity, tok_dev), 0).astype(jnp.float32)
    for e in range(0, experts, 2):
        here, gate_here = [], []
        for f in (e, e + 1):
            mask = jnp.broadcast_to(rank[f : f + 1, :], (capacity, tok_dev)) == slots
            here.append(jnp.where(mask, 1.0, 0.0))
            gate_here.append(
                jnp.where(mask, jnp.broadcast_to(gate[f : f + 1, :], (capacity, tok_dev)), 0.0)
            )
        span = slice(e * capacity, (e + 2) * capacity)
        place[0, span, :] = jnp.concatenate(here, axis=0).astype(place.dtype)
        place[1, span, :] = jnp.concatenate(gate_here, axis=0).astype(place.dtype)

    half = shards.shape[1] // 2
    shard_copies = [
        [
            pltpu.make_async_copy(
                shards.at[k, pl.ds(c * half, half), :],
                out.at[pl.ds(k * half, half), :],
                shard_sems.at[k, c],
            )
            for c, out in enumerate((shard_a_hbm, shard_b_hbm))
        ]
        for k in range(3)
    ]
    steps = width // PACK_COLS

    def out_copy(i):
        cols = (slice(None), pl.ds(pl.multiple_of(i * PACK_COLS, PACK_COLS), PACK_COLS))
        return pltpu.make_async_copy(packed.at[cols], packed_hbm.at[cols], out_sems.at[i])

    for k in range(2):
        row_copies[k].wait()

        @pl.loop(0, steps)
        def _(i):
            source = pl.ds(pl.multiple_of(i * PACK_COLS, PACK_COLS), PACK_COLS)
            target = pl.ds(pl.multiple_of((k * steps + i) * PACK_COLS, PACK_COLS), PACK_COLS)
            packed[:, target] = matmul(place[k], tokens[k, :, source]).astype(packed.dtype)
            out_copy(k * steps + i).start()

        if k == 0:
            for m in range(3):
                w_copies[m].wait()
                if m == 2:
                    shards[2] = down[...].T
                for copy in shard_copies[m]:
                    copy.start()
    for copy in sum(shard_copies, [out_copy(i) for i in range(2 * steps)]):
        copy.wait()


def pack(routes, gate_values, tokens, cotangent, w_gate, w_up, w_down, experts, capacity):
    tok_dev, width = tokens.shape
    slots = experts * capacity
    vmem = pl.BlockSpec(memory_space=pltpu.VMEM)
    hbm = pl.BlockSpec(memory_space=pl.ANY)
    return pl.pallas_call(
        lambda *refs: pack_kernel(capacity, *refs),
        in_specs=[vmem] * 2 + [hbm] * 5,
        out_specs=[hbm, vmem, hbm, hbm],
        out_shape=[
            jax.ShapeDtypeStruct((slots, 2 * width), tokens.dtype),
            jax.ShapeDtypeStruct((experts, tok_dev), jnp.int32),
            *[jax.ShapeDtypeStruct((3 * w_gate.shape[1] // 2, w_gate.shape[2]), w_gate.dtype)] * 2,
        ],
        scratch_shapes=[
            pltpu.VMEM((2, tok_dev, width), tokens.dtype),
            pltpu.VMEM((3, *w_gate.shape[1:]), w_gate.dtype),
            pltpu.VMEM(w_down.shape[1:], w_down.dtype),
            pltpu.VMEM((2, slots, tok_dev), jnp.bfloat16),
            pltpu.VMEM((slots, 2 * width), tokens.dtype),
            pltpu.SemaphoreType.DMA((2,)),
            pltpu.SemaphoreType.DMA((3,)),
            pltpu.SemaphoreType.DMA((3, 2)),
            pltpu.SemaphoreType.DMA((2 * width // PACK_COLS,)),
        ],
        compiler_params=pltpu.CompilerParams(vmem_limit_bytes=60 << 20),
        cost_estimate=pl.CostEstimate(
            flops=4 * slots * tok_dev * width,
            bytes_accessed=4 * slots * width,
            transcendentals=0,
        ),
        name="pack",
    )(routes.T, gate_values.T, tokens, cotangent, w_gate, w_up, w_down)


def first_hops(n):
    far, near = n // 2, (n - 1) // 2
    return (far, near), (n - near, n - far)


def later_hops(n):
    sent = {(k, c) for pair in first_hops(n) for c, k in enumerate(pair)}
    return [(k, c) for k in range(n) for c in range(2) if (k, c) not in sent]


def block_terms(k, chains, me, parts, rows, grads, hidden_t, store):
    width = rows.shape[1] // 2
    ff = hidden_t.shape[0]
    block = width // parts
    half = block // 2
    start = lax.rem(me + k, parts) * block
    if len(chains) == 2:
        x_cols = rows[:, pl.ds(pl.multiple_of(start, block), block)]
    else:
        x_cols = rows[:, pl.ds(pl.multiple_of(start + chains[0] * half, half), half)]
    s_cols = rows[:, pl.ds(pl.multiple_of(width + start, block), block)]
    both = matmul(x_cols, grads[...], ((0,), (0,))).astype(jnp.bfloat16)
    if len(chains) == 2:
        down = matmul(hidden_t[...], s_cols).astype(jnp.bfloat16)
    for i, c in enumerate(chains):
        span = slice(i * half, (i + 1) * half)
        store(c, slice(0, half), slice(0, ff), both[span, :ff])
        store(c, slice(half, 2 * half), slice(0, ff), both[span, ff:])
        for h in range(ff // block):
            feature = slice(h * block + c * half, h * block + (c + 1) * half)
            if len(chains) == 2:
                value = down[feature]
            else:
                value = matmul(hidden_t[feature, :], s_cols).astype(jnp.bfloat16)
            store(c, slice(2 * half, 3 * half), slice(h * block, (h + 1) * block), value)


def terms_kernel(parts, me_ref, rows_hbm, *refs):
    pieces, refs = refs[: 2 * parts], refs[2 * parts :]
    grads_hbm, hidden_hbm, w_hbm, refs = refs[0], refs[1], refs[2], refs[3:]
    firsts, refs = refs[:2], refs[2:]
    rows, w, grads, hidden_t, terms, row_sems, w_sems, keep_sems, out_sems = refs
    _, width, ff = w.shape
    n = rows.shape[0]
    block = width // parts
    half = block // 2
    me = me_ref[0]

    def row_copy(k, left, size):
        span = (pl.ds(k * ROWS, ROWS), pl.ds(left, size))
        return pltpu.make_async_copy(
            rows_hbm.at[span], rows.at[span], row_sems.at[k + (1 if left else 0) + (k > 0)]
        )

    def w_copy(m, k, c):
        start = pl.multiple_of(lax.rem(me + parts - k, parts) * block + c * half, half)
        return pltpu.make_async_copy(
            pieces[2 * k + c].at[pl.ds(m * half, half), :],
            w.at[m, pl.ds(start, half), :],
            w_sems.at[m, k, c],
        )

    x_copy = row_copy(0, 0, width)
    scaled_copy = row_copy(0, width, width)
    later = [row_copy(k, 0, 2 * width) for k in range(1, n // ROWS)]
    w_copies = [[w_copy(m, k, c) for k in range(parts) for c in range(2)] for m in range(3)]
    for copy in [x_copy, *w_copies[0], *w_copies[1], scaled_copy, *w_copies[2], *later]:
        copy.start()
    keep = [
        pltpu.make_async_copy(grads, grads_hbm, keep_sems.at[0]),
        pltpu.make_async_copy(hidden_t, hidden_hbm, keep_sems.at[1]),
        pltpu.make_async_copy(w.at[pl.ds(0, 2)], w_hbm, keep_sems.at[2]),
    ]

    for k in range(n // ROWS):
        span = slice(k * ROWS, (k + 1) * ROWS)
        if k == 0:
            x_copy.wait()
            for copy in w_copies[0]:
                copy.wait()
        else:
            later[k - 1].wait()
        x = rows[span, :width]
        gate_pre = matmul(x, w[0])
        sig = 1.0 / (1.0 + jnp.exp(-gate_pre))
        activated = gate_pre * sig
        slope = sig * (1.0 + gate_pre * (1.0 - sig))
        if k == 0:
            for copy in w_copies[1]:
                copy.wait()
        up_pre = matmul(x, w[1])
        hidden_t[:, span] = (activated * up_pre).astype(jnp.bfloat16).T
        if k == 0:
            scaled_copy.wait()
            for copy in w_copies[2]:
                copy.wait()
        hidden_grad = matmul(rows[span, width:], w[2])
        grads[span, :ff] = (hidden_grad * up_pre * slope).astype(jnp.bfloat16)
        grads[span, ff:] = (hidden_grad * activated).astype(jnp.bfloat16)
        if k == 0:
            keep[2].start()

    keep[0].start()
    keep[1].start()
    hops = first_hops(parts)
    wanted = {}
    for d, pair in enumerate(hops):
        for c, k in enumerate(pair):
            wanted.setdefault(k, {})[c] = d
    for k, chains in wanted.items():

        def store(c, r, f, value):
            terms[chains[c], c * 3 * half + r.start : c * 3 * half + r.stop, f] = value

        block_terms(k, sorted(chains), me, parts, rows, grads, hidden_t, store)
    out_copies = [pltpu.make_async_copy(terms.at[d], firsts[d], out_sems.at[d]) for d in range(2)]
    for copy in out_copies:
        copy.start()
    for copy in [*keep, *out_copies]:
        copy.wait()


def terms_of(me, received, pieces):
    rows, width2 = received.shape
    width = width2 // 2
    parts = len(pieces) // 2
    piece_rows, ff = pieces[0].shape
    hbm = pl.BlockSpec(memory_space=pl.ANY)
    grads, hidden_t, w_in, *first = pl.pallas_call(
        lambda *refs: terms_kernel(parts, *refs),
        in_specs=[pl.BlockSpec(memory_space=pltpu.SMEM)] + [hbm] * (1 + 2 * parts),
        out_specs=[hbm] * 5,
        out_shape=[
            jax.ShapeDtypeStruct((rows, 2 * ff), jnp.bfloat16),
            jax.ShapeDtypeStruct((ff, rows), jnp.bfloat16),
            jax.ShapeDtypeStruct((2, width, ff), jnp.bfloat16),
            *[jax.ShapeDtypeStruct((2 * piece_rows, ff), jnp.bfloat16)] * 2,
        ],
        scratch_shapes=[
            pltpu.VMEM((rows, width2), jnp.bfloat16),
            pltpu.VMEM((3, width, ff), jnp.bfloat16),
            pltpu.VMEM((rows, 2 * ff), jnp.bfloat16),
            pltpu.VMEM((ff, rows), jnp.bfloat16),
            pltpu.VMEM((2, 2 * piece_rows, ff), jnp.bfloat16),
            pltpu.SemaphoreType.DMA((1 + rows // ROWS,)),
            pltpu.SemaphoreType.DMA((3, parts, 2)),
            pltpu.SemaphoreType.DMA((3,)),
            pltpu.SemaphoreType.DMA((2,)),
        ],
        compiler_params=pltpu.CompilerParams(vmem_limit_bytes=60 << 20),
        cost_estimate=pl.CostEstimate(
            flops=8 * rows * width * ff,
            bytes_accessed=2 * (2 * rows * width + 6 * width * ff),
            transcendentals=rows * ff,
        ),
        name="terms",
    )(me, received, *pieces)
    row_grad, *own = pl.pallas_call(
        lambda *refs: rest_kernel(parts, *refs),
        in_specs=[pl.BlockSpec(memory_space=pltpu.SMEM)] + [hbm] * 4,
        out_specs=[hbm] * (1 + len(later_hops(parts))),
        out_shape=[
            jax.ShapeDtypeStruct((rows, width), jnp.bfloat16),
            *[jax.ShapeDtypeStruct((piece_rows, ff), jnp.bfloat16)] * len(later_hops(parts)),
        ],
        scratch_shapes=[
            pltpu.VMEM((rows, width2), jnp.bfloat16),
            pltpu.VMEM((2, width, ff), jnp.bfloat16),
            pltpu.VMEM((rows, 2 * ff), jnp.bfloat16),
            pltpu.VMEM((ff, rows), jnp.bfloat16),
            pltpu.VMEM((rows, width), jnp.bfloat16),
            pltpu.VMEM((parts, 2, piece_rows, ff), jnp.bfloat16),
            pltpu.SemaphoreType.DMA((4,)),
            pltpu.SemaphoreType.DMA((width // TERM_COLS,)),
            pltpu.SemaphoreType.DMA((parts, 2)),
        ],
        compiler_params=pltpu.CompilerParams(vmem_limit_bytes=60 << 20),
        cost_estimate=pl.CostEstimate(
            flops=8 * rows * width * ff,
            bytes_accessed=2 * (3 * rows * width + 5 * width * ff),
            transcendentals=0,
        ),
        name="rest",
    )(me, received, grads, hidden_t, w_in)
    return row_grad, dict(zip(later_hops(parts), own)), first


def rest_kernel(parts, me_ref, rows_hbm, grads_hbm, hidden_hbm, w_hbm, row_grad_hbm, *refs):
    later = later_hops(parts)
    outs, refs = refs[: len(later)], refs[len(later) :]
    rows, w, grads, hidden_t, row_grad, terms, in_sems, row_sems, out_sems = refs
    _, width, ff = w.shape
    me = me_ref[0]
    sources = [grads_hbm, w_hbm, hidden_hbm, rows_hbm]
    targets = [grads, w, hidden_t, rows]
    arrive = [
        pltpu.make_async_copy(a, b, in_sems.at[k]) for k, (a, b) in enumerate(zip(sources, targets))
    ]
    for copy in arrive:
        copy.start()
    arrive[0].wait()
    arrive[1].wait()
    leave = []
    for k, start in enumerate(range(0, width, TERM_COLS)):
        span = slice(start, start + TERM_COLS)
        value = matmul(grads[:, :ff], w[0, span, :], ((1,), (1,)))
        value = value + matmul(grads[:, ff:], w[1, span, :], ((1,), (1,)))
        row_grad[:, span] = value.astype(jnp.bfloat16)
        cols = (slice(None), pl.ds(start, TERM_COLS))
        leave.append(pltpu.make_async_copy(row_grad.at[cols], row_grad_hbm.at[cols], row_sems.at[k]))
        leave[-1].start()
    arrive[2].wait()
    arrive[3].wait()
    for k in range(parts):

        def store(c, r, f, value):
            terms[k, c, r, f] = value

        chains = [c for c in range(2) if (k, c) in later]
        if chains:
            block_terms(k, chains, me, parts, rows, grads, hidden_t, store)
        for c in chains:
            out = outs[later.index((k, c))]
            leave.append(pltpu.make_async_copy(terms.at[k, c], out, out_sems.at[k, c]))
            leave[-1].start()
    for copy in leave:
        copy.wait()


def finish_kernel(own_a, right_a, left_a, own_b, right_b, left_b, gate_ref, up_ref, down_ref):
    half = own_a.shape[0] // 3
    block = 2 * half
    for c, (own, right, left) in enumerate(((own_a, right_a, left_a), (own_b, right_b, left_b))):
        total = (
            own[...].astype(jnp.float32)
            + right[...].astype(jnp.float32)
            + left[...].astype(jnp.float32)
        ).astype(gate_ref.dtype)
        span = slice(c * half, (c + 1) * half)
        gate_ref[0, span, :] = total[:half]
        up_ref[0, span, :] = total[half : 2 * half]
        for h in range(total.shape[1] // block):
            down_ref[0, h * block + c * half : h * block + (c + 1) * half, :] = total[
                2 * half :, h * block : (h + 1) * block
            ]


def finish(*parts):
    piece_rows, ff = parts[0].shape
    rows = 2 * piece_rows // 3
    vmem = pl.BlockSpec(memory_space=pltpu.VMEM)
    return pl.pallas_call(
        finish_kernel,
        in_specs=[vmem] * 6,
        out_specs=[vmem] * 3,
        out_shape=[
            jax.ShapeDtypeStruct((1, rows, ff), parts[0].dtype),
            jax.ShapeDtypeStruct((1, rows, ff), parts[0].dtype),
            jax.ShapeDtypeStruct((1, ff, rows), parts[0].dtype),
        ],
        compiler_params=pltpu.CompilerParams(vmem_limit_bytes=60 << 20),
        name="finish",
    )(*parts)


def shift(a, by):
    n = lax.axis_size("dp")
    return lax.ppermute(a, "dp", [(i, (i + by) % n) for i in range(n)])


def ring_gather(shard, far):
    n = lax.axis_size("dp")
    moved = {1: [shard], -1: [shard]}
    for by in (far, -far):
        for _ in range(n // 2 if by == far else (n - 1) // 2):
            moved[by].append(shift(moved[by][-1], by))
    right, left = moved[1], moved[-1]
    return [right[k] if k < len(right) else left[n - k] for k in range(n)]


def ring_scatter(own, first, n):
    half = first[0].shape[0] // 2
    arrived = {
        (c, by): a[c * half : (c + 1) * half]
        for a, by in zip(first, (1, -1))
        for c in range(2)
    }
    left = {
        (c, by): hops[c] if by > 0 else n - hops[c]
        for hops, by in zip(first_hops(n), (1, -1))
        for c in range(2)
    }
    for _ in range(n // 2):
        for (c, by), hops in left.items():
            if hops > 1:
                left[c, by] = hops - 1
                mine = own[by * (hops - 1) % n, c].astype(jnp.float32)
                total = arrived[c, by].astype(jnp.float32) + mine
                arrived[c, by] = shift(total.astype(jnp.bfloat16), by)
    return [a for c in range(2) for a in (own[0, c], arrived[c, 1], arrived[c, -1])]


def local(tokens, cotangent, routes, gate_values, w_gate, w_up, w_down):
    experts = lax.axis_size("expert")
    tok_dev, model_width = tokens.shape
    fan_out = routes.shape[1]
    capacity = min(tok_dev, 3 * tok_dev * fan_out // (2 * experts))

    def exchange(rows):
        return lax.all_to_all(
            rows.reshape(experts, capacity, rows.shape[1]),
            "expert",
            split_axis=0,
            concat_axis=0,
            tiled=True,
        ).reshape(rows.shape)

    packed, rank, shard_a, shard_b = pack(
        routes, gate_values, tokens, cotangent, w_gate, w_up, w_down, experts, capacity
    )
    received = exchange(packed)
    pieces_a, pieces_b = ring_gather(shard_a, 1), ring_gather(shard_b, -1)
    pieces = [p for pair in zip(pieces_a, pieces_b) for p in pair]
    me = lax.axis_index("dp").astype(jnp.int32).reshape(1)
    row_grad, own, first = terms_of(me, received, pieces)
    hops = [shift(a, by) for a, by in zip(first, (1, -1))]
    row_grad, *hops = lax.optimization_barrier((row_grad, *hops))
    sums = ring_scatter(own, hops, lax.axis_size("dp"))

    returned = exchange(row_grad)
    place = rank[:, None, :] == jnp.arange(capacity, dtype=jnp.int32)[None, :, None]
    place = place.reshape(experts * capacity, tok_dev).astype(jnp.bfloat16)
    token_grad = matmul(place, returned, ((0,), (0,))).astype(jnp.bfloat16)
    return (token_grad, *finish(*sums))


def solution(mesh):
    in_specs = (
        P(("expert", "dp"), None),
        P(("expert", "dp"), None),
        P(("expert", "dp"), None),
        P(("expert", "dp"), None),
        P("expert", "dp", None),
        P("expert", "dp", None),
        P("expert", None, "dp"),
    )
    out_specs = (
        P(("expert", "dp"), None),
        P("expert", "dp", None),
        P("expert", "dp", None),
        P("expert", None, "dp"),
    )
    return jax.shard_map(local, mesh=mesh, in_specs=in_specs, out_specs=out_specs, check_vma=False)
```

```python
import jax
import jax.numpy as jnp
from jax import lax
from jax.experimental import pallas as pl
from jax.experimental.pallas import tpu as pltpu
from jax.sharding import PartitionSpec as P

ROWS = 384
COLS = 256
TERM_COLS = 512
PACK_COLS = 512


def matmul(a, b, dims=((1,), (0,))):
    return lax.dot_general(a, b, (dims, ((), ())), preferred_element_type=jnp.float32)


def pack_kernel(
    capacity,
    routes_ref,
    gate_ref,
    tokens_hbm,
    cotangent_hbm,
    w_gate_hbm,
    w_up_hbm,
    w_down_hbm,
    packed_hbm,
    rank_ref,
    shard_a_hbm,
    shard_b_hbm,
    tokens,
    shards,
    down,
    place,
    packed,
    in_sems,
    w_sems,
    shard_sems,
    out_sems,
):
    experts, tok_dev = rank_ref.shape
    width = tokens_hbm.shape[1]
    sources = [tokens_hbm, cotangent_hbm]
    row_copies = [
        pltpu.make_async_copy(sources[k], tokens.at[k], in_sems.at[k]) for k in range(2)
    ]
    w_copies = [
        pltpu.make_async_copy(w_gate_hbm.at[0], shards.at[0], w_sems.at[0]),
        pltpu.make_async_copy(w_up_hbm.at[0], shards.at[1], w_sems.at[1]),
        pltpu.make_async_copy(w_down_hbm.at[0], down, w_sems.at[2]),
    ]
    for copy in row_copies + w_copies:
        copy.start()

    ids = lax.broadcasted_iota(jnp.int32, (experts, tok_dev), 0)
    gates = gate_ref[...].astype(jnp.float32)
    member = jnp.zeros((experts, tok_dev), jnp.float32)
    gate = jnp.zeros((experts, tok_dev), jnp.float32)
    for k in range(routes_ref.shape[0]):
        hit = routes_ref[k : k + 1, :] == ids
        member = jnp.where(hit, 1.0, member)
        gate = jnp.where(hit, gates[k : k + 1, :], gate)
    row = lax.broadcasted_iota(jnp.int32, (tok_dev, tok_dev), 0)
    col = lax.broadcasted_iota(jnp.int32, (tok_dev, tok_dev), 1)
    before = matmul(member.astype(jnp.bfloat16), (row < col).astype(jnp.bfloat16))
    rank = jnp.where(member > 0.5, before, -1.0)
    rank_ref[...] = rank.astype(jnp.int32)
    slots = lax.broadcasted_iota(jnp.int32, (capacity, tok_dev), 0).astype(jnp.float32)
    for e in range(0, experts, 2):
        here, gate_here = [], []
        for f in (e, e + 1):
            mask = jnp.broadcast_to(rank[f : f + 1, :], (capacity, tok_dev)) == slots
            here.append(jnp.where(mask, 1.0, 0.0))
            gate_here.append(
                jnp.where(mask, jnp.broadcast_to(gate[f : f + 1, :], (capacity, tok_dev)), 0.0)
            )
        span = slice(e * capacity, (e + 2) * capacity)
        place[0, span, :] = jnp.concatenate(here, axis=0).astype(place.dtype)
        place[1, span, :] = jnp.concatenate(gate_here, axis=0).astype(place.dtype)

    half = shards.shape[1] // 2
    shard_copies = [
        [
            pltpu.make_async_copy(
                shards.at[k, pl.ds(c * half, half), :],
                out.at[pl.ds(k * half, half), :],
                shard_sems.at[k, c],
            )
            for c, out in enumerate((shard_a_hbm, shard_b_hbm))
        ]
        for k in range(3)
    ]
    steps = width // PACK_COLS

    def out_copy(i):
        cols = (slice(None), pl.ds(pl.multiple_of(i * PACK_COLS, PACK_COLS), PACK_COLS))
        return pltpu.make_async_copy(packed.at[cols], packed_hbm.at[cols], out_sems.at[i])

    for k in range(2):
        row_copies[k].wait()

        @pl.loop(0, steps)
        def _(i):
            source = pl.ds(pl.multiple_of(i * PACK_COLS, PACK_COLS), PACK_COLS)
            target = pl.ds(pl.multiple_of((k * steps + i) * PACK_COLS, PACK_COLS), PACK_COLS)
            packed[:, target] = matmul(place[k], tokens[k, :, source]).astype(packed.dtype)
            out_copy(k * steps + i).start()

        if k == 0:
            for m in range(3):
                w_copies[m].wait()
                if m == 2:
                    shards[2] = down[...].T
                for copy in shard_copies[m]:
                    copy.start()
    for copy in sum(shard_copies, [out_copy(i) for i in range(2 * steps)]):
        copy.wait()


def pack(routes, gate_values, tokens, cotangent, w_gate, w_up, w_down, experts, capacity):
    tok_dev, width = tokens.shape
    slots = experts * capacity
    vmem = pl.BlockSpec(memory_space=pltpu.VMEM)
    hbm = pl.BlockSpec(memory_space=pl.ANY)
    return pl.pallas_call(
        lambda *refs: pack_kernel(capacity, *refs),
        in_specs=[vmem] * 2 + [hbm] * 5,
        out_specs=[hbm, vmem, hbm, hbm],
        out_shape=[
            jax.ShapeDtypeStruct((slots, 2 * width), tokens.dtype),
            jax.ShapeDtypeStruct((experts, tok_dev), jnp.int32),
            *[jax.ShapeDtypeStruct((3 * w_gate.shape[1] // 2, w_gate.shape[2]), w_gate.dtype)] * 2,
        ],
        scratch_shapes=[
            pltpu.VMEM((2, tok_dev, width), tokens.dtype),
            pltpu.VMEM((3, *w_gate.shape[1:]), w_gate.dtype),
            pltpu.VMEM(w_down.shape[1:], w_down.dtype),
            pltpu.VMEM((2, slots, tok_dev), jnp.bfloat16),
            pltpu.VMEM((slots, 2 * width), tokens.dtype),
            pltpu.SemaphoreType.DMA((2,)),
            pltpu.SemaphoreType.DMA((3,)),
            pltpu.SemaphoreType.DMA((3, 2)),
            pltpu.SemaphoreType.DMA((2 * width // PACK_COLS,)),
        ],
        compiler_params=pltpu.CompilerParams(vmem_limit_bytes=60 << 20),
        cost_estimate=pl.CostEstimate(
            flops=4 * slots * tok_dev * width,
            bytes_accessed=4 * slots * width,
            transcendentals=0,
        ),
        name="pack",
    )(routes.T, gate_values.T, tokens, cotangent, w_gate, w_up, w_down)


def first_hops(n):
    far, near = n // 2, (n - 1) // 2
    return (far, near), (n - near, n - far)


def later_hops(n):
    sent = {(k, c) for pair in first_hops(n) for c, k in enumerate(pair)}
    return [(k, c) for k in range(n) for c in range(2) if (k, c) not in sent]


def block_terms(k, chains, me, parts, rows, grads, hidden_t, store):
    width = rows.shape[1] // 2
    ff = hidden_t.shape[0]
    block = width // parts
    half = block // 2
    start = lax.rem(me + k, parts) * block
    if len(chains) == 2:
        x_cols = rows[:, pl.ds(pl.multiple_of(start, block), block)]
    else:
        x_cols = rows[:, pl.ds(pl.multiple_of(start + chains[0] * half, half), half)]
    s_cols = rows[:, pl.ds(pl.multiple_of(width + start, block), block)]
    both = matmul(x_cols, grads[...], ((0,), (0,))).astype(jnp.bfloat16)
    if len(chains) == 2:
        down = matmul(hidden_t[...], s_cols).astype(jnp.bfloat16)
    for i, c in enumerate(chains):
        span = slice(i * half, (i + 1) * half)
        store(c, slice(0, half), slice(0, ff), both[span, :ff])
        store(c, slice(half, 2 * half), slice(0, ff), both[span, ff:])
        for h in range(ff // block):
            feature = slice(h * block + c * half, h * block + (c + 1) * half)
            if len(chains) == 2:
                value = down[feature]
            else:
                value = matmul(hidden_t[feature, :], s_cols).astype(jnp.bfloat16)
            store(c, slice(2 * half, 3 * half), slice(h * block, (h + 1) * block), value)


def terms_kernel(parts, me_ref, rows_hbm, *refs):
    pieces, refs = refs[: 2 * parts], refs[2 * parts :]
    grads_hbm, hidden_hbm, w_hbm, refs = refs[0], refs[1], refs[2], refs[3:]
    firsts, refs = refs[:2], refs[2:]
    rows, w, grads, hidden_t, terms, row_sems, w_sems, keep_sems, out_sems = refs
    _, width, ff = w.shape
    n = rows.shape[0]
    block = width // parts
    half = block // 2
    me = me_ref[0]

    def row_copy(k, left, size):
        span = (pl.ds(k * ROWS, ROWS), pl.ds(left, size))
        return pltpu.make_async_copy(
            rows_hbm.at[span], rows.at[span], row_sems.at[k + (1 if left else 0) + (k > 0)]
        )

    def w_copy(m, k, c):
        start = pl.multiple_of(lax.rem(me + parts - k, parts) * block + c * half, half)
        return pltpu.make_async_copy(
            pieces[2 * k + c].at[pl.ds(m * half, half), :],
            w.at[m, pl.ds(start, half), :],
            w_sems.at[m, k, c],
        )

    x_copy = row_copy(0, 0, width)
    scaled_copy = row_copy(0, width, width)
    later = [row_copy(k, 0, 2 * width) for k in range(1, n // ROWS)]
    w_copies = [[w_copy(m, k, c) for k in range(parts) for c in range(2)] for m in range(3)]
    for copy in [x_copy, *w_copies[0], *w_copies[1], scaled_copy, *w_copies[2], *later]:
        copy.start()
    keep = [
        pltpu.make_async_copy(grads, grads_hbm, keep_sems.at[0]),
        pltpu.make_async_copy(hidden_t, hidden_hbm, keep_sems.at[1]),
        pltpu.make_async_copy(w.at[pl.ds(0, 2)], w_hbm, keep_sems.at[2]),
    ]

    for k in range(n // ROWS):
        span = slice(k * ROWS, (k + 1) * ROWS)
        if k == 0:
            x_copy.wait()
            for copy in w_copies[0]:
                copy.wait()
        else:
            later[k - 1].wait()
        x = rows[span, :width]
        gate_pre = matmul(x, w[0])
        sig = 1.0 / (1.0 + jnp.exp(-gate_pre))
        activated = gate_pre * sig
        slope = sig * (1.0 + gate_pre * (1.0 - sig))
        if k == 0:
            for copy in w_copies[1]:
                copy.wait()
        up_pre = matmul(x, w[1])
        hidden_t[:, span] = (activated * up_pre).astype(jnp.bfloat16).T
        if k == 0:
            scaled_copy.wait()
            for copy in w_copies[2]:
                copy.wait()
        hidden_grad = matmul(rows[span, width:], w[2])
        grads[span, :ff] = (hidden_grad * up_pre * slope).astype(jnp.bfloat16)
        grads[span, ff:] = (hidden_grad * activated).astype(jnp.bfloat16)
        if k == 0:
            keep[2].start()

    keep[0].start()
    keep[1].start()
    hops = first_hops(parts)
    wanted = {}
    for d, pair in enumerate(hops):
        for c, k in enumerate(pair):
            wanted.setdefault(k, {})[c] = d
    for k, chains in wanted.items():

        def store(c, r, f, value):
            terms[chains[c], c * 3 * half + r.start : c * 3 * half + r.stop, f] = value

        block_terms(k, sorted(chains), me, parts, rows, grads, hidden_t, store)
    out_copies = [pltpu.make_async_copy(terms.at[d], firsts[d], out_sems.at[d]) for d in range(2)]
    for copy in out_copies:
        copy.start()
    for copy in [*keep, *out_copies]:
        copy.wait()


def terms_of(me, received, pieces):
    rows, width2 = received.shape
    width = width2 // 2
    parts = len(pieces) // 2
    piece_rows, ff = pieces[0].shape
    hbm = pl.BlockSpec(memory_space=pl.ANY)
    grads, hidden_t, w_in, *first = pl.pallas_call(
        lambda *refs: terms_kernel(parts, *refs),
        in_specs=[pl.BlockSpec(memory_space=pltpu.SMEM)] + [hbm] * (1 + 2 * parts),
        out_specs=[hbm] * 5,
        out_shape=[
            jax.ShapeDtypeStruct((rows, 2 * ff), jnp.bfloat16),
            jax.ShapeDtypeStruct((ff, rows), jnp.bfloat16),
            jax.ShapeDtypeStruct((2, width, ff), jnp.bfloat16),
            *[jax.ShapeDtypeStruct((2 * piece_rows, ff), jnp.bfloat16)] * 2,
        ],
        scratch_shapes=[
            pltpu.VMEM((rows, width2), jnp.bfloat16),
            pltpu.VMEM((3, width, ff), jnp.bfloat16),
            pltpu.VMEM((rows, 2 * ff), jnp.bfloat16),
            pltpu.VMEM((ff, rows), jnp.bfloat16),
            pltpu.VMEM((2, 2 * piece_rows, ff), jnp.bfloat16),
            pltpu.SemaphoreType.DMA((1 + rows // ROWS,)),
            pltpu.SemaphoreType.DMA((3, parts, 2)),
            pltpu.SemaphoreType.DMA((3,)),
            pltpu.SemaphoreType.DMA((2,)),
        ],
        compiler_params=pltpu.CompilerParams(vmem_limit_bytes=60 << 20),
        cost_estimate=pl.CostEstimate(
            flops=8 * rows * width * ff,
            bytes_accessed=2 * (2 * rows * width + 6 * width * ff),
            transcendentals=rows * ff,
        ),
        name="terms",
    )(me, received, *pieces)
    row_grad, *own = pl.pallas_call(
        lambda *refs: rest_kernel(parts, *refs),
        in_specs=[pl.BlockSpec(memory_space=pltpu.SMEM)] + [hbm] * 4,
        out_specs=[hbm] * (1 + len(later_hops(parts))),
        out_shape=[
            jax.ShapeDtypeStruct((rows, width), jnp.bfloat16),
            *[jax.ShapeDtypeStruct((piece_rows, ff), jnp.bfloat16)] * len(later_hops(parts)),
        ],
        scratch_shapes=[
            pltpu.VMEM((rows, width2), jnp.bfloat16),
            pltpu.VMEM((2, width, ff), jnp.bfloat16),
            pltpu.VMEM((rows, 2 * ff), jnp.bfloat16),
            pltpu.VMEM((ff, rows), jnp.bfloat16),
            pltpu.VMEM((rows, width), jnp.bfloat16),
            pltpu.VMEM((parts, 2, piece_rows, ff), jnp.bfloat16),
            pltpu.SemaphoreType.DMA((4,)),
            pltpu.SemaphoreType.DMA((width // TERM_COLS,)),
            pltpu.SemaphoreType.DMA((parts, 2)),
        ],
        compiler_params=pltpu.CompilerParams(vmem_limit_bytes=60 << 20),
        cost_estimate=pl.CostEstimate(
            flops=8 * rows * width * ff,
            bytes_accessed=2 * (3 * rows * width + 5 * width * ff),
            transcendentals=0,
        ),
        name="rest",
    )(me, received, grads, hidden_t, w_in)
    return row_grad, dict(zip(later_hops(parts), own)), first


def rest_kernel(parts, me_ref, rows_hbm, grads_hbm, hidden_hbm, w_hbm, row_grad_hbm, *refs):
    later = later_hops(parts)
    outs, refs = refs[: len(later)], refs[len(later) :]
    rows, w, grads, hidden_t, row_grad, terms, in_sems, row_sems, out_sems = refs
    _, width, ff = w.shape
    me = me_ref[0]
    sources = [grads_hbm, w_hbm, hidden_hbm, rows_hbm]
    targets = [grads, w, hidden_t, rows]
    arrive = [
        pltpu.make_async_copy(a, b, in_sems.at[k]) for k, (a, b) in enumerate(zip(sources, targets))
    ]
    for copy in arrive:
        copy.start()
    arrive[0].wait()
    arrive[1].wait()
    leave = []
    def row_copy(i):
        cols = (slice(None), pl.ds(pl.multiple_of(i * TERM_COLS, TERM_COLS), TERM_COLS))
        return pltpu.make_async_copy(row_grad.at[cols], row_grad_hbm.at[cols], row_sems.at[i])

    @pl.loop(0, width // TERM_COLS)
    def _(i):
        span = pl.ds(pl.multiple_of(i * TERM_COLS, TERM_COLS), TERM_COLS)
        value = matmul(grads[:, :ff], w[0, span, :], ((1,), (1,)))
        value = value + matmul(grads[:, ff:], w[1, span, :], ((1,), (1,)))
        row_grad[:, span] = value.astype(jnp.bfloat16)
        row_copy(i).start()

    leave += [row_copy(i) for i in range(width // TERM_COLS)]
    arrive[2].wait()
    arrive[3].wait()
    out_copies = {
        (k, c): pltpu.make_async_copy(terms.at[k, c], out, out_sems.at[k, c])
        for (k, c), out in zip(later, outs)
    }
    whole = [k for k in range(parts) if (k, 0) in later and (k, 1) in later]
    first = parts - (parts - 1) // 2 + 1

    def fill(k, chains):
        def store(c, r, f, value):
            terms[k, c, r, f] = value

        block_terms(k, chains, me, parts, rows, grads, hidden_t, store)

    for k, c in later:
        if k not in whole:
            fill(k, [c])
            out_copies[k, c].start()

    @pl.loop(0, len(whole))
    def _(i):
        k = lax.rem(first + i, parts)
        fill(k, [0, 1])
        for j in whole:

            @pl.when(k == j)
            def _():
                out_copies[j, 0].start()
                out_copies[j, 1].start()

    leave += list(out_copies.values())
    for copy in leave:
        copy.wait()


def finish_kernel(own_a, right_a, left_a, own_b, right_b, left_b, gate_ref, up_ref, down_ref):
    half = own_a.shape[0] // 3
    block = 2 * half
    for c, (own, right, left) in enumerate(((own_a, right_a, left_a), (own_b, right_b, left_b))):
        total = (
            own[...].astype(jnp.float32)
            + right[...].astype(jnp.float32)
            + left[...].astype(jnp.float32)
        ).astype(gate_ref.dtype)
        span = slice(c * half, (c + 1) * half)
        gate_ref[0, span, :] = total[:half]
        up_ref[0, span, :] = total[half : 2 * half]
        for h in range(total.shape[1] // block):
            down_ref[0, h * block + c * half : h * block + (c + 1) * half, :] = total[
                2 * half :, h * block : (h + 1) * block
            ]


def finish(*parts):
    piece_rows, ff = parts[0].shape
    rows = 2 * piece_rows // 3
    vmem = pl.BlockSpec(memory_space=pltpu.VMEM)
    return pl.pallas_call(
        finish_kernel,
        in_specs=[vmem] * 6,
        out_specs=[vmem] * 3,
        out_shape=[
            jax.ShapeDtypeStruct((1, rows, ff), parts[0].dtype),
            jax.ShapeDtypeStruct((1, rows, ff), parts[0].dtype),
            jax.ShapeDtypeStruct((1, ff, rows), parts[0].dtype),
        ],
        compiler_params=pltpu.CompilerParams(vmem_limit_bytes=60 << 20),
        name="finish",
    )(*parts)


def shift(a, by):
    n = lax.axis_size("dp")
    return lax.ppermute(a, "dp", [(i, (i + by) % n) for i in range(n)])


def ring_gather(shard, far):
    n = lax.axis_size("dp")
    moved = {1: [shard], -1: [shard]}
    for by in (far, -far):
        for _ in range(n // 2 if by == far else (n - 1) // 2):
            moved[by].append(shift(moved[by][-1], by))
    right, left = moved[1], moved[-1]
    return [right[k] if k < len(right) else left[n - k] for k in range(n)]


def ring_scatter(own, first, n):
    half = first[0].shape[0] // 2
    arrived = {
        (c, by): a[c * half : (c + 1) * half]
        for a, by in zip(first, (1, -1))
        for c in range(2)
    }
    left = {
        (c, by): hops[c] if by > 0 else n - hops[c]
        for hops, by in zip(first_hops(n), (1, -1))
        for c in range(2)
    }
    for _ in range(n // 2):
        for c in range(2):
            going = [by for by in (1, -1) if left[c, by] > 1]
            for by in going:
                left[c, by] -= 1
                mine = own[by * left[c, by] % n, c].astype(jnp.float32)
                total = arrived[c, by].astype(jnp.float32) + mine
                arrived[c, by] = shift(total.astype(jnp.bfloat16), by)
            if len(going) == 2:
                arrived[c, 1], arrived[c, -1] = lax.optimization_barrier(
                    (arrived[c, 1], arrived[c, -1])
                )
    return [a for c in range(2) for a in (own[0, c], arrived[c, 1], arrived[c, -1])]


def local(tokens, cotangent, routes, gate_values, w_gate, w_up, w_down):
    experts = lax.axis_size("expert")
    tok_dev, model_width = tokens.shape
    fan_out = routes.shape[1]
    capacity = min(tok_dev, 3 * tok_dev * fan_out // (2 * experts))

    def exchange(rows):
        return lax.all_to_all(
            rows.reshape(experts, capacity, rows.shape[1]),
            "expert",
            split_axis=0,
            concat_axis=0,
            tiled=True,
        ).reshape(rows.shape)

    packed, rank, shard_a, shard_b = pack(
        routes, gate_values, tokens, cotangent, w_gate, w_up, w_down, experts, capacity
    )
    received = exchange(packed)
    pieces_a, pieces_b = ring_gather(shard_a, 1), ring_gather(shard_b, -1)
    pieces = [p for pair in zip(pieces_a, pieces_b) for p in pair]
    me = lax.axis_index("dp").astype(jnp.int32).reshape(1)
    row_grad, own, first = terms_of(me, received, pieces)
    hops = [shift(a, by) for a, by in zip(first, (1, -1))]
    hops = lax.optimization_barrier(hops)
    sums = ring_scatter(own, hops, lax.axis_size("dp"))

    returned = exchange(row_grad)
    place = rank[:, None, :] == jnp.arange(capacity, dtype=jnp.int32)[None, :, None]
    place = place.reshape(experts * capacity, tok_dev).astype(jnp.bfloat16)
    token_grad = matmul(place, returned, ((0,), (0,))).astype(jnp.bfloat16)
    return (token_grad, *finish(*sums))


def solution(mesh):
    in_specs = (
        P(("expert", "dp"), None),
        P(("expert", "dp"), None),
        P(("expert", "dp"), None),
        P(("expert", "dp"), None),
        P("expert", "dp", None),
        P("expert", "dp", None),
        P("expert", None, "dp"),
    )
    out_specs = (
        P(("expert", "dp"), None),
        P("expert", "dp", None),
        P("expert", "dp", None),
        P("expert", None, "dp"),
    )
    return jax.shard_map(local, mesh=mesh, in_specs=in_specs, out_specs=out_specs, check_vma=False)
```

```python
import jax
import jax.numpy as jnp
from jax import lax
from jax.experimental import pallas as pl
from jax.experimental.pallas import tpu as pltpu
from jax.sharding import PartitionSpec as P

ROWS = 384
COLS = 256
TERM_COLS = 512
PACK_COLS = 512


def matmul(a, b, dims=((1,), (0,))):
    return lax.dot_general(a, b, (dims, ((), ())), preferred_element_type=jnp.float32)


def pack_kernel(
    capacity,
    routes_ref,
    gate_ref,
    tokens_hbm,
    cotangent_hbm,
    w_gate_hbm,
    w_up_hbm,
    w_down_hbm,
    packed_hbm,
    rank_ref,
    shard_a_hbm,
    shard_b_hbm,
    tokens,
    shards,
    down,
    place,
    packed,
    in_sems,
    w_sems,
    shard_sems,
    out_sems,
):
    experts, tok_dev = rank_ref.shape
    width = tokens_hbm.shape[1]
    sources = [tokens_hbm, cotangent_hbm]
    row_copies = [
        pltpu.make_async_copy(sources[k], tokens.at[k], in_sems.at[k]) for k in range(2)
    ]
    w_copies = [
        pltpu.make_async_copy(w_gate_hbm.at[0], shards.at[0], w_sems.at[0]),
        pltpu.make_async_copy(w_up_hbm.at[0], shards.at[1], w_sems.at[1]),
        pltpu.make_async_copy(w_down_hbm.at[0], down, w_sems.at[2]),
    ]
    for copy in row_copies + w_copies:
        copy.start()

    ids = lax.broadcasted_iota(jnp.int32, (experts, tok_dev), 0)
    gates = gate_ref[...].astype(jnp.float32)
    member = jnp.zeros((experts, tok_dev), jnp.float32)
    gate = jnp.zeros((experts, tok_dev), jnp.float32)
    for k in range(routes_ref.shape[0]):
        hit = routes_ref[k : k + 1, :] == ids
        member = jnp.where(hit, 1.0, member)
        gate = jnp.where(hit, gates[k : k + 1, :], gate)
    row = lax.broadcasted_iota(jnp.int32, (tok_dev, tok_dev), 0)
    col = lax.broadcasted_iota(jnp.int32, (tok_dev, tok_dev), 1)
    before = matmul(member.astype(jnp.bfloat16), (row < col).astype(jnp.bfloat16))
    rank = jnp.where(member > 0.5, before, -1.0)
    rank_ref[...] = rank.astype(jnp.int32)
    slots = lax.broadcasted_iota(jnp.int32, (capacity, tok_dev), 0).astype(jnp.float32)
    for e in range(0, experts, 2):
        here, gate_here = [], []
        for f in (e, e + 1):
            mask = jnp.broadcast_to(rank[f : f + 1, :], (capacity, tok_dev)) == slots
            here.append(jnp.where(mask, 1.0, 0.0))
            gate_here.append(
                jnp.where(mask, jnp.broadcast_to(gate[f : f + 1, :], (capacity, tok_dev)), 0.0)
            )
        span = slice(e * capacity, (e + 2) * capacity)
        place[0, span, :] = jnp.concatenate(here, axis=0).astype(place.dtype)
        place[1, span, :] = jnp.concatenate(gate_here, axis=0).astype(place.dtype)

    half = shards.shape[1] // 2
    shard_copies = [
        [
            pltpu.make_async_copy(
                shards.at[k, pl.ds(c * half, half), :],
                out.at[pl.ds(k * half, half), :],
                shard_sems.at[k, c],
            )
            for c, out in enumerate((shard_a_hbm, shard_b_hbm))
        ]
        for k in range(3)
    ]
    steps = width // PACK_COLS

    def out_copy(i):
        cols = (slice(None), pl.ds(i * PACK_COLS, PACK_COLS))
        return pltpu.make_async_copy(packed.at[cols], packed_hbm.at[cols], out_sems.at[i])

    for k in range(2):
        row_copies[k].wait()

        for i in range(steps):
            source = pl.ds(i * PACK_COLS, PACK_COLS)
            target = pl.ds((k * steps + i) * PACK_COLS, PACK_COLS)
            packed[:, target] = matmul(place[k], tokens[k, :, source]).astype(packed.dtype)
            out_copy(k * steps + i).start()

        if k == 0:
            for m in range(3):
                w_copies[m].wait()
                if m == 2:
                    shards[2] = down[...].T
                for copy in shard_copies[m]:
                    copy.start()
    for copy in sum(shard_copies, [out_copy(i) for i in range(2 * steps)]):
        copy.wait()


def pack(routes, gate_values, tokens, cotangent, w_gate, w_up, w_down, experts, capacity):
    tok_dev, width = tokens.shape
    slots = experts * capacity
    vmem = pl.BlockSpec(memory_space=pltpu.VMEM)
    hbm = pl.BlockSpec(memory_space=pl.ANY)
    return pl.pallas_call(
        lambda *refs: pack_kernel(capacity, *refs),
        in_specs=[vmem] * 2 + [hbm] * 5,
        out_specs=[hbm, vmem, hbm, hbm],
        out_shape=[
            jax.ShapeDtypeStruct((slots, 2 * width), tokens.dtype),
            jax.ShapeDtypeStruct((experts, tok_dev), jnp.int32),
            *[jax.ShapeDtypeStruct((3 * w_gate.shape[1] // 2, w_gate.shape[2]), w_gate.dtype)] * 2,
        ],
        scratch_shapes=[
            pltpu.VMEM((2, tok_dev, width), tokens.dtype),
            pltpu.VMEM((3, *w_gate.shape[1:]), w_gate.dtype),
            pltpu.VMEM(w_down.shape[1:], w_down.dtype),
            pltpu.VMEM((2, slots, tok_dev), jnp.bfloat16),
            pltpu.VMEM((slots, 2 * width), tokens.dtype),
            pltpu.SemaphoreType.DMA((2,)),
            pltpu.SemaphoreType.DMA((3,)),
            pltpu.SemaphoreType.DMA((3, 2)),
            pltpu.SemaphoreType.DMA((2 * width // PACK_COLS,)),
        ],
        compiler_params=pltpu.CompilerParams(vmem_limit_bytes=60 << 20),
        cost_estimate=pl.CostEstimate(
            flops=4 * slots * tok_dev * width,
            bytes_accessed=4 * slots * width,
            transcendentals=0,
        ),
        name="pack",
    )(routes.T, gate_values.T, tokens, cotangent, w_gate, w_up, w_down)


def first_hops(n):
    far, near = n // 2, (n - 1) // 2
    return (far, near), (n - near, n - far)


def later_hops(n):
    sent = {(k, c) for pair in first_hops(n) for c, k in enumerate(pair)}
    return [(k, c) for k in range(n) for c in range(2) if (k, c) not in sent]


def block_terms(k, chains, me, parts, rows, grads, hidden_t, store):
    width = rows.shape[1] // 2
    ff = hidden_t.shape[0]
    block = width // parts
    half = block // 2
    start = lax.rem(me + k, parts) * block
    if len(chains) == 2:
        x_cols = rows[:, pl.ds(pl.multiple_of(start, block), block)]
    else:
        x_cols = rows[:, pl.ds(pl.multiple_of(start + chains[0] * half, half), half)]
    s_cols = rows[:, pl.ds(pl.multiple_of(width + start, block), block)]
    both = matmul(x_cols, grads[...], ((0,), (0,))).astype(jnp.bfloat16)
    if len(chains) == 2:
        down = matmul(hidden_t[...], s_cols).astype(jnp.bfloat16)
    for i, c in enumerate(chains):
        span = slice(i * half, (i + 1) * half)
        store(c, slice(0, half), slice(0, ff), both[span, :ff])
        store(c, slice(half, 2 * half), slice(0, ff), both[span, ff:])
        for h in range(ff // block):
            feature = slice(h * block + c * half, h * block + (c + 1) * half)
            if len(chains) == 2:
                value = down[feature]
            else:
                value = matmul(hidden_t[feature, :], s_cols).astype(jnp.bfloat16)
            store(c, slice(2 * half, 3 * half), slice(h * block, (h + 1) * block), value)


def terms_kernel(parts, me_ref, rows_hbm, *refs):
    pieces, refs = refs[: 2 * parts], refs[2 * parts :]
    grads_hbm, hidden_hbm, w_hbm, refs = refs[0], refs[1], refs[2], refs[3:]
    firsts, refs = refs[:2], refs[2:]
    rows, w, grads, hidden_t, terms, row_sems, w_sems, keep_sems, out_sems = refs
    _, width, ff = w.shape
    n = rows.shape[0]
    block = width // parts
    half = block // 2
    me = me_ref[0]

    def row_copy(k, left, size):
        span = (pl.ds(k * ROWS, ROWS), pl.ds(left, size))
        return pltpu.make_async_copy(
            rows_hbm.at[span], rows.at[span], row_sems.at[k + (1 if left else 0) + (k > 0)]
        )

    def w_copy(m, k, c):
        start = pl.multiple_of(lax.rem(me + parts - k, parts) * block + c * half, half)
        return pltpu.make_async_copy(
            pieces[2 * k + c].at[pl.ds(m * half, half), :],
            w.at[m, pl.ds(start, half), :],
            w_sems.at[m, k, c],
        )

    x_copy = row_copy(0, 0, width)
    scaled_copy = row_copy(0, width, width)
    later = [row_copy(k, 0, 2 * width) for k in range(1, n // ROWS)]
    w_copies = [[w_copy(m, k, c) for k in range(parts) for c in range(2)] for m in range(3)]
    for copy in [x_copy, *w_copies[0], *w_copies[1], scaled_copy, *w_copies[2], *later]:
        copy.start()
    keep = [
        pltpu.make_async_copy(grads, grads_hbm, keep_sems.at[0]),
        pltpu.make_async_copy(hidden_t, hidden_hbm, keep_sems.at[1]),
        pltpu.make_async_copy(w.at[pl.ds(0, 2)], w_hbm, keep_sems.at[2]),
    ]

    for k in range(n // ROWS):
        span = slice(k * ROWS, (k + 1) * ROWS)
        if k == 0:
            x_copy.wait()
            for copy in w_copies[0]:
                copy.wait()
        else:
            later[k - 1].wait()
        x = rows[span, :width]
        gate_pre = matmul(x, w[0])
        sig = 1.0 / (1.0 + jnp.exp(-gate_pre))
        activated = gate_pre * sig
        slope = sig * (1.0 + gate_pre * (1.0 - sig))
        if k == 0:
            for copy in w_copies[1]:
                copy.wait()
        up_pre = matmul(x, w[1])
        hidden_t[:, span] = (activated * up_pre).astype(jnp.bfloat16).T
        if k == 0:
            scaled_copy.wait()
            for copy in w_copies[2]:
                copy.wait()
        hidden_grad = matmul(rows[span, width:], w[2])
        grads[span, :ff] = (hidden_grad * up_pre * slope).astype(jnp.bfloat16)
        grads[span, ff:] = (hidden_grad * activated).astype(jnp.bfloat16)
        if k == 0:
            keep[2].start()

    keep[0].start()
    keep[1].start()
    hops = first_hops(parts)
    wanted = {}
    for d, pair in enumerate(hops):
        for c, k in enumerate(pair):
            wanted.setdefault(k, {})[c] = d
    for k, chains in wanted.items():

        def store(c, r, f, value):
            terms[chains[c], c * 3 * half + r.start : c * 3 * half + r.stop, f] = value

        block_terms(k, sorted(chains), me, parts, rows, grads, hidden_t, store)
    out_copies = [pltpu.make_async_copy(terms.at[d], firsts[d], out_sems.at[d]) for d in range(2)]
    for copy in out_copies:
        copy.start()
    for copy in [*keep, *out_copies]:
        copy.wait()


def terms_of(me, received, pieces):
    rows, width2 = received.shape
    width = width2 // 2
    parts = len(pieces) // 2
    piece_rows, ff = pieces[0].shape
    hbm = pl.BlockSpec(memory_space=pl.ANY)
    grads, hidden_t, w_in, *first = pl.pallas_call(
        lambda *refs: terms_kernel(parts, *refs),
        in_specs=[pl.BlockSpec(memory_space=pltpu.SMEM)] + [hbm] * (1 + 2 * parts),
        out_specs=[hbm] * 5,
        out_shape=[
            jax.ShapeDtypeStruct((rows, 2 * ff), jnp.bfloat16),
            jax.ShapeDtypeStruct((ff, rows), jnp.bfloat16),
            jax.ShapeDtypeStruct((2, width, ff), jnp.bfloat16),
            *[jax.ShapeDtypeStruct((2 * piece_rows, ff), jnp.bfloat16)] * 2,
        ],
        scratch_shapes=[
            pltpu.VMEM((rows, width2), jnp.bfloat16),
            pltpu.VMEM((3, width, ff), jnp.bfloat16),
            pltpu.VMEM((rows, 2 * ff), jnp.bfloat16),
            pltpu.VMEM((ff, rows), jnp.bfloat16),
            pltpu.VMEM((2, 2 * piece_rows, ff), jnp.bfloat16),
            pltpu.SemaphoreType.DMA((1 + rows // ROWS,)),
            pltpu.SemaphoreType.DMA((3, parts, 2)),
            pltpu.SemaphoreType.DMA((3,)),
            pltpu.SemaphoreType.DMA((2,)),
        ],
        compiler_params=pltpu.CompilerParams(vmem_limit_bytes=60 << 20),
        cost_estimate=pl.CostEstimate(
            flops=8 * rows * width * ff,
            bytes_accessed=2 * (2 * rows * width + 6 * width * ff),
            transcendentals=rows * ff,
        ),
        name="terms",
    )(me, received, *pieces)
    row_grad, *own = pl.pallas_call(
        lambda *refs: rest_kernel(parts, *refs),
        in_specs=[pl.BlockSpec(memory_space=pltpu.SMEM)] + [hbm] * 4,
        out_specs=[hbm] * (1 + len(later_hops(parts))),
        out_shape=[
            jax.ShapeDtypeStruct((rows, width), jnp.bfloat16),
            *[jax.ShapeDtypeStruct((piece_rows, ff), jnp.bfloat16)] * len(later_hops(parts)),
        ],
        scratch_shapes=[
            pltpu.VMEM((rows, width2), jnp.bfloat16),
            pltpu.VMEM((2, width, ff), jnp.bfloat16),
            pltpu.VMEM((rows, 2 * ff), jnp.bfloat16),
            pltpu.VMEM((ff, rows), jnp.bfloat16),
            pltpu.VMEM((rows, width), jnp.bfloat16),
            pltpu.VMEM((parts, 2, piece_rows, ff), jnp.bfloat16),
            pltpu.SemaphoreType.DMA((4,)),
            pltpu.SemaphoreType.DMA((width // TERM_COLS,)),
            pltpu.SemaphoreType.DMA((parts, 2)),
        ],
        compiler_params=pltpu.CompilerParams(vmem_limit_bytes=60 << 20),
        cost_estimate=pl.CostEstimate(
            flops=8 * rows * width * ff,
            bytes_accessed=2 * (3 * rows * width + 5 * width * ff),
            transcendentals=0,
        ),
        name="rest",
    )(me, received, grads, hidden_t, w_in)
    return row_grad, dict(zip(later_hops(parts), own)), first


def rest_kernel(parts, me_ref, rows_hbm, grads_hbm, hidden_hbm, w_hbm, row_grad_hbm, *refs):
    later = later_hops(parts)
    outs, refs = refs[: len(later)], refs[len(later) :]
    rows, w, grads, hidden_t, row_grad, terms, in_sems, row_sems, out_sems = refs
    _, width, ff = w.shape
    me = me_ref[0]
    sources = [grads_hbm, w_hbm, hidden_hbm, rows_hbm]
    targets = [grads, w, hidden_t, rows]
    arrive = [
        pltpu.make_async_copy(a, b, in_sems.at[k]) for k, (a, b) in enumerate(zip(sources, targets))
    ]
    for copy in arrive:
        copy.start()
    arrive[0].wait()
    arrive[1].wait()
    leave = []
    def row_copy(i):
        cols = (slice(None), pl.ds(pl.multiple_of(i * TERM_COLS, TERM_COLS), TERM_COLS))
        return pltpu.make_async_copy(row_grad.at[cols], row_grad_hbm.at[cols], row_sems.at[i])

    @pl.loop(0, width // TERM_COLS)
    def _(i):
        span = pl.ds(pl.multiple_of(i * TERM_COLS, TERM_COLS), TERM_COLS)
        value = matmul(grads[:, :ff], w[0, span, :], ((1,), (1,)))
        value = value + matmul(grads[:, ff:], w[1, span, :], ((1,), (1,)))
        row_grad[:, span] = value.astype(jnp.bfloat16)
        row_copy(i).start()

    leave += [row_copy(i) for i in range(width // TERM_COLS)]
    arrive[2].wait()
    arrive[3].wait()
    out_copies = {
        (k, c): pltpu.make_async_copy(terms.at[k, c], out, out_sems.at[k, c])
        for (k, c), out in zip(later, outs)
    }
    whole = [k for k in range(parts) if (k, 0) in later and (k, 1) in later]
    first = parts - (parts - 1) // 2 + 1

    def fill(k, chains):
        def store(c, r, f, value):
            terms[k, c, r, f] = value

        block_terms(k, chains, me, parts, rows, grads, hidden_t, store)

    for k, c in later:
        if k not in whole:
            fill(k, [c])
            out_copies[k, c].start()

    @pl.loop(0, len(whole))
    def _(i):
        k = lax.rem(first + i, parts)
        fill(k, [0, 1])
        for j in whole:

            @pl.when(k == j)
            def _():
                out_copies[j, 0].start()
                out_copies[j, 1].start()

    leave += list(out_copies.values())
    for copy in leave:
        copy.wait()


def finish_kernel(own_a, right_a, left_a, own_b, right_b, left_b, gate_ref, up_ref, down_ref):
    half = own_a.shape[0] // 3
    block = 2 * half
    for c, (own, right, left) in enumerate(((own_a, right_a, left_a), (own_b, right_b, left_b))):
        total = (
            own[...].astype(jnp.float32)
            + right[...].astype(jnp.float32)
            + left[...].astype(jnp.float32)
        ).astype(gate_ref.dtype)
        span = slice(c * half, (c + 1) * half)
        gate_ref[0, span, :] = total[:half]
        up_ref[0, span, :] = total[half : 2 * half]
        for h in range(total.shape[1] // block):
            down_ref[0, h * block + c * half : h * block + (c + 1) * half, :] = total[
                2 * half :, h * block : (h + 1) * block
            ]


def finish(*parts):
    piece_rows, ff = parts[0].shape
    rows = 2 * piece_rows // 3
    vmem = pl.BlockSpec(memory_space=pltpu.VMEM)
    return pl.pallas_call(
        finish_kernel,
        in_specs=[vmem] * 6,
        out_specs=[vmem] * 3,
        out_shape=[
            jax.ShapeDtypeStruct((1, rows, ff), parts[0].dtype),
            jax.ShapeDtypeStruct((1, rows, ff), parts[0].dtype),
            jax.ShapeDtypeStruct((1, ff, rows), parts[0].dtype),
        ],
        compiler_params=pltpu.CompilerParams(vmem_limit_bytes=60 << 20),
        name="finish",
    )(*parts)


def shift(a, by):
    n = lax.axis_size("dp")
    return lax.ppermute(a, "dp", [(i, (i + by) % n) for i in range(n)])


def ring_gather(shard, far):
    n = lax.axis_size("dp")
    moved = {1: [shard], -1: [shard]}
    for by in (far, -far):
        for _ in range(n // 2 if by == far else (n - 1) // 2):
            moved[by].append(shift(moved[by][-1], by))
    right, left = moved[1], moved[-1]
    return [right[k] if k < len(right) else left[n - k] for k in range(n)]


def ring_scatter(own, first, n):
    half = first[0].shape[0] // 2
    arrived = {
        (c, by): a[c * half : (c + 1) * half]
        for a, by in zip(first, (1, -1))
        for c in range(2)
    }
    left = {
        (c, by): hops[c] if by > 0 else n - hops[c]
        for hops, by in zip(first_hops(n), (1, -1))
        for c in range(2)
    }
    for _ in range(n // 2):
        for c in range(2):
            going = [by for by in (1, -1) if left[c, by] > 1]
            for by in going:
                left[c, by] -= 1
                mine = own[by * left[c, by] % n, c].astype(jnp.float32)
                total = arrived[c, by].astype(jnp.float32) + mine
                arrived[c, by] = shift(total.astype(jnp.bfloat16), by)
            if len(going) == 2:
                arrived[c, 1], arrived[c, -1] = lax.optimization_barrier(
                    (arrived[c, 1], arrived[c, -1])
                )
    return [a for c in range(2) for a in (own[0, c], arrived[c, 1], arrived[c, -1])]


def local(tokens, cotangent, routes, gate_values, w_gate, w_up, w_down):
    experts = lax.axis_size("expert")
    tok_dev, model_width = tokens.shape
    fan_out = routes.shape[1]
    capacity = min(tok_dev, 3 * tok_dev * fan_out // (2 * experts))

    def exchange(rows):
        return lax.all_to_all(
            rows.reshape(experts, capacity, rows.shape[1]),
            "expert",
            split_axis=0,
            concat_axis=0,
            tiled=True,
        ).reshape(rows.shape)

    packed, rank, shard_a, shard_b = pack(
        routes, gate_values, tokens, cotangent, w_gate, w_up, w_down, experts, capacity
    )
    received = exchange(packed)
    pieces_a, pieces_b = ring_gather(shard_a, 1), ring_gather(shard_b, -1)
    pieces = [p for pair in zip(pieces_a, pieces_b) for p in pair]
    me = lax.axis_index("dp").astype(jnp.int32).reshape(1)
    row_grad, own, first = terms_of(me, received, pieces)
    hops = [shift(a, by) for a, by in zip(first, (1, -1))]
    hops = lax.optimization_barrier(hops)
    sums = ring_scatter(own, hops, lax.axis_size("dp"))

    returned = exchange(row_grad)
    place = rank[:, None, :] == jnp.arange(capacity, dtype=jnp.int32)[None, :, None]
    place = place.reshape(experts * capacity, tok_dev).astype(jnp.bfloat16)
    token_grad = matmul(place, returned, ((0,), (0,))).astype(jnp.bfloat16)
    token_grad, *sums = lax.optimization_barrier((token_grad, *sums))
    return (token_grad, *finish(*sums))


def solution(mesh):
    in_specs = (
        P(("expert", "dp"), None),
        P(("expert", "dp"), None),
        P(("expert", "dp"), None),
        P(("expert", "dp"), None),
        P("expert", "dp", None),
        P("expert", "dp", None),
        P("expert", None, "dp"),
    )
    out_specs = (
        P(("expert", "dp"), None),
        P("expert", "dp", None),
        P("expert", "dp", None),
        P("expert", None, "dp"),
    )
    return jax.shard_map(local, mesh=mesh, in_specs=in_specs, out_specs=out_specs, check_vma=False)
```

```python
import jax
import jax.numpy as jnp
from jax import lax
from jax.experimental import pallas as pl
from jax.experimental.pallas import tpu as pltpu
from jax.sharding import PartitionSpec as P

ROWS = 384
COLS = 256
TERM_COLS = 512
PACK_COLS = 512


def matmul(a, b, dims=((1,), (0,))):
    return lax.dot_general(a, b, (dims, ((), ())), preferred_element_type=jnp.float32)


def pack_kernel(
    capacity,
    routes_ref,
    gate_ref,
    tokens_hbm,
    cotangent_hbm,
    w_gate_hbm,
    w_up_hbm,
    w_down_hbm,
    packed_hbm,
    rank_ref,
    shard_a_hbm,
    shard_b_hbm,
    tokens,
    shards,
    down,
    place,
    packed,
    in_sems,
    w_sems,
    shard_sems,
    out_sems,
):
    experts, tok_dev = rank_ref.shape
    width = tokens_hbm.shape[1]
    sources = [tokens_hbm, cotangent_hbm]
    row_copies = [
        pltpu.make_async_copy(sources[k], tokens.at[k], in_sems.at[k]) for k in range(2)
    ]
    w_copies = [
        pltpu.make_async_copy(w_gate_hbm.at[0], shards.at[0], w_sems.at[0]),
        pltpu.make_async_copy(w_up_hbm.at[0], shards.at[1], w_sems.at[1]),
        pltpu.make_async_copy(w_down_hbm.at[0], down, w_sems.at[2]),
    ]
    for copy in row_copies + w_copies:
        copy.start()

    ids = lax.broadcasted_iota(jnp.int32, (experts, tok_dev), 0)
    gates = gate_ref[...].astype(jnp.float32)
    member = jnp.zeros((experts, tok_dev), jnp.float32)
    gate = jnp.zeros((experts, tok_dev), jnp.float32)
    for k in range(routes_ref.shape[0]):
        hit = routes_ref[k : k + 1, :] == ids
        member = jnp.where(hit, 1.0, member)
        gate = jnp.where(hit, gates[k : k + 1, :], gate)
    row = lax.broadcasted_iota(jnp.int32, (tok_dev, tok_dev), 0)
    col = lax.broadcasted_iota(jnp.int32, (tok_dev, tok_dev), 1)
    before = matmul(member.astype(jnp.bfloat16), (row < col).astype(jnp.bfloat16))
    rank = jnp.where(member > 0.5, before, -1.0)
    rank_ref[...] = rank.astype(jnp.int32)
    slots = lax.broadcasted_iota(jnp.int32, (capacity, tok_dev), 0).astype(jnp.float32)
    for e in range(0, experts, 2):
        here, gate_here = [], []
        for f in (e, e + 1):
            mask = jnp.broadcast_to(rank[f : f + 1, :], (capacity, tok_dev)) == slots
            here.append(jnp.where(mask, 1.0, 0.0))
            gate_here.append(
                jnp.where(mask, jnp.broadcast_to(gate[f : f + 1, :], (capacity, tok_dev)), 0.0)
            )
        span = slice(e * capacity, (e + 2) * capacity)
        place[0, span, :] = jnp.concatenate(here, axis=0).astype(place.dtype)
        place[1, span, :] = jnp.concatenate(gate_here, axis=0).astype(place.dtype)

    half = shards.shape[1] // 2
    shard_copies = [
        [
            pltpu.make_async_copy(
                shards.at[k, pl.ds(c * half, half), :],
                out.at[pl.ds(k * half, half), :],
                shard_sems.at[k, c],
            )
            for c, out in enumerate((shard_a_hbm, shard_b_hbm))
        ]
        for k in range(3)
    ]
    steps = width // PACK_COLS

    def out_copy(i):
        cols = (slice(None), pl.ds(i * PACK_COLS, PACK_COLS))
        return pltpu.make_async_copy(packed.at[cols], packed_hbm.at[cols], out_sems.at[i])

    for k in range(2):
        row_copies[k].wait()

        for i in range(steps):
            source = pl.ds(i * PACK_COLS, PACK_COLS)
            target = pl.ds((k * steps + i) * PACK_COLS, PACK_COLS)
            packed[:, target] = matmul(place[k], tokens[k, :, source]).astype(packed.dtype)
            out_copy(k * steps + i).start()

        if k == 0:
            for m in range(3):
                w_copies[m].wait()
                if m == 2:
                    shards[2] = down[...].T
                for copy in shard_copies[m]:
                    copy.start()
    for copy in sum(shard_copies, [out_copy(i) for i in range(2 * steps)]):
        copy.wait()


def pack(routes, gate_values, tokens, cotangent, w_gate, w_up, w_down, experts, capacity):
    tok_dev, width = tokens.shape
    slots = experts * capacity
    vmem = pl.BlockSpec(memory_space=pltpu.VMEM)
    hbm = pl.BlockSpec(memory_space=pl.ANY)
    return pl.pallas_call(
        lambda *refs: pack_kernel(capacity, *refs),
        in_specs=[vmem] * 2 + [hbm] * 5,
        out_specs=[hbm, vmem, hbm, hbm],
        out_shape=[
            jax.ShapeDtypeStruct((slots, 2 * width), tokens.dtype),
            jax.ShapeDtypeStruct((experts, tok_dev), jnp.int32),
            *[jax.ShapeDtypeStruct((3 * w_gate.shape[1] // 2, w_gate.shape[2]), w_gate.dtype)] * 2,
        ],
        scratch_shapes=[
            pltpu.VMEM((2, tok_dev, width), tokens.dtype),
            pltpu.VMEM((3, *w_gate.shape[1:]), w_gate.dtype),
            pltpu.VMEM(w_down.shape[1:], w_down.dtype),
            pltpu.VMEM((2, slots, tok_dev), jnp.bfloat16),
            pltpu.VMEM((slots, 2 * width), tokens.dtype),
            pltpu.SemaphoreType.DMA((2,)),
            pltpu.SemaphoreType.DMA((3,)),
            pltpu.SemaphoreType.DMA((3, 2)),
            pltpu.SemaphoreType.DMA((2 * width // PACK_COLS,)),
        ],
        compiler_params=pltpu.CompilerParams(vmem_limit_bytes=60 << 20),
        cost_estimate=pl.CostEstimate(
            flops=4 * slots * tok_dev * width,
            bytes_accessed=4 * slots * width,
            transcendentals=0,
        ),
        name="pack",
    )(routes.T, gate_values.T, tokens, cotangent, w_gate, w_up, w_down)


def first_hops(n):
    far, near = n // 2, (n - 1) // 2
    return (far, near), (n - near, n - far)


def later_hops(n):
    sent = {(k, c) for pair in first_hops(n) for c, k in enumerate(pair)}
    return [(k, c) for k in range(n) for c in range(2) if (k, c) not in sent]


def block_terms(k, chains, me, parts, rows, grads, hidden_t, store):
    width = rows.shape[1] // 2
    ff = hidden_t.shape[0]
    block = width // parts
    half = block // 2
    start = lax.rem(me + k, parts) * block
    if len(chains) == 2:
        x_cols = rows[:, pl.ds(pl.multiple_of(start, block), block)]
    else:
        x_cols = rows[:, pl.ds(pl.multiple_of(start + chains[0] * half, half), half)]
    s_cols = rows[:, pl.ds(pl.multiple_of(width + start, block), block)]
    both = matmul(x_cols, grads[...], ((0,), (0,))).astype(jnp.bfloat16)
    if len(chains) == 2:
        down = matmul(hidden_t[...], s_cols).astype(jnp.bfloat16)
    for i, c in enumerate(chains):
        span = slice(i * half, (i + 1) * half)
        store(c, slice(0, half), slice(0, ff), both[span, :ff])
        store(c, slice(half, 2 * half), slice(0, ff), both[span, ff:])
        for h in range(ff // block):
            feature = slice(h * block + c * half, h * block + (c + 1) * half)
            if len(chains) == 2:
                value = down[feature]
            else:
                value = matmul(hidden_t[feature, :], s_cols).astype(jnp.bfloat16)
            store(c, slice(2 * half, 3 * half), slice(h * block, (h + 1) * block), value)


def terms_kernel(parts, me_ref, rows_hbm, *refs):
    pieces, refs = refs[: 2 * parts], refs[2 * parts :]
    grads_hbm, hidden_hbm, w_hbm, refs = refs[0], refs[1], refs[2], refs[3:]
    firsts, refs = refs[:2], refs[2:]
    rows, w, grads, hidden_t, terms, row_sems, w_sems, keep_sems, out_sems = refs
    _, width, ff = w.shape
    n = rows.shape[0]
    block = width // parts
    half = block // 2
    me = me_ref[0]

    def row_copy(k, left, size):
        span = (pl.ds(k * ROWS, ROWS), pl.ds(left, size))
        return pltpu.make_async_copy(
            rows_hbm.at[span], rows.at[span], row_sems.at[k + (1 if left else 0) + (k > 0)]
        )

    def w_copy(m, k, c):
        start = pl.multiple_of(lax.rem(me + parts - k, parts) * block + c * half, half)
        return pltpu.make_async_copy(
            pieces[2 * k + c].at[pl.ds(m * half, half), :],
            w.at[m, pl.ds(start, half), :],
            w_sems.at[m, k, c],
        )

    x_copy = row_copy(0, 0, width)
    scaled_copy = row_copy(0, width, width)
    later = [row_copy(k, 0, 2 * width) for k in range(1, n // ROWS)]
    w_copies = [[w_copy(m, k, c) for k in range(parts) for c in range(2)] for m in range(3)]
    for copy in [x_copy, *w_copies[0], *w_copies[1], scaled_copy, *w_copies[2], *later]:
        copy.start()
    keep = [
        pltpu.make_async_copy(grads, grads_hbm, keep_sems.at[0]),
        pltpu.make_async_copy(hidden_t, hidden_hbm, keep_sems.at[1]),
        pltpu.make_async_copy(w.at[pl.ds(0, 2)], w_hbm, keep_sems.at[2]),
    ]

    for k in range(n // ROWS):
        span = slice(k * ROWS, (k + 1) * ROWS)
        if k == 0:
            x_copy.wait()
            for copy in w_copies[0]:
                copy.wait()
        else:
            later[k - 1].wait()
        x = rows[span, :width]
        gate_pre = matmul(x, w[0])
        sig = 1.0 / (1.0 + jnp.exp(-gate_pre))
        activated = gate_pre * sig
        slope = sig * (1.0 + gate_pre * (1.0 - sig))
        if k == 0:
            for copy in w_copies[1]:
                copy.wait()
        up_pre = matmul(x, w[1])
        hidden_t[:, span] = (activated * up_pre).astype(jnp.bfloat16).T
        if k == 0:
            scaled_copy.wait()
            for copy in w_copies[2]:
                copy.wait()
        hidden_grad = matmul(rows[span, width:], w[2])
        grads[span, :ff] = (hidden_grad * up_pre * slope).astype(jnp.bfloat16)
        grads[span, ff:] = (hidden_grad * activated).astype(jnp.bfloat16)
        if k == 0:
            keep[2].start()

    keep[0].start()
    keep[1].start()
    hops = first_hops(parts)
    wanted = {}
    for d, pair in enumerate(hops):
        for c, k in enumerate(pair):
            wanted.setdefault(k, {})[c] = d
    for k, chains in wanted.items():

        def store(c, r, f, value):
            terms[chains[c], c * 3 * half + r.start : c * 3 * half + r.stop, f] = value

        block_terms(k, sorted(chains), me, parts, rows, grads, hidden_t, store)
    out_copies = [pltpu.make_async_copy(terms.at[d], firsts[d], out_sems.at[d]) for d in range(2)]
    for copy in out_copies:
        copy.start()
    for copy in [*keep, *out_copies]:
        copy.wait()


def terms_of(me, received, pieces):
    rows, width2 = received.shape
    width = width2 // 2
    parts = len(pieces) // 2
    piece_rows, ff = pieces[0].shape
    hbm = pl.BlockSpec(memory_space=pl.ANY)
    grads, hidden_t, w_in, *first = pl.pallas_call(
        lambda *refs: terms_kernel(parts, *refs),
        in_specs=[pl.BlockSpec(memory_space=pltpu.SMEM)] + [hbm] * (1 + 2 * parts),
        out_specs=[hbm] * 5,
        out_shape=[
            jax.ShapeDtypeStruct((rows, 2 * ff), jnp.bfloat16),
            jax.ShapeDtypeStruct((ff, rows), jnp.bfloat16),
            jax.ShapeDtypeStruct((2, width, ff), jnp.bfloat16),
            *[jax.ShapeDtypeStruct((2 * piece_rows, ff), jnp.bfloat16)] * 2,
        ],
        scratch_shapes=[
            pltpu.VMEM((rows, width2), jnp.bfloat16),
            pltpu.VMEM((3, width, ff), jnp.bfloat16),
            pltpu.VMEM((rows, 2 * ff), jnp.bfloat16),
            pltpu.VMEM((ff, rows), jnp.bfloat16),
            pltpu.VMEM((2, 2 * piece_rows, ff), jnp.bfloat16),
            pltpu.SemaphoreType.DMA((1 + rows // ROWS,)),
            pltpu.SemaphoreType.DMA((3, parts, 2)),
            pltpu.SemaphoreType.DMA((3,)),
            pltpu.SemaphoreType.DMA((2,)),
        ],
        compiler_params=pltpu.CompilerParams(vmem_limit_bytes=60 << 20),
        cost_estimate=pl.CostEstimate(
            flops=8 * rows * width * ff,
            bytes_accessed=2 * (2 * rows * width + 6 * width * ff),
            transcendentals=rows * ff,
        ),
        name="terms",
    )(me, received, *pieces)
    row_grad, *own = pl.pallas_call(
        lambda *refs: rest_kernel(parts, *refs),
        in_specs=[pl.BlockSpec(memory_space=pltpu.SMEM)] + [hbm] * 4,
        out_specs=[hbm] * (1 + len(later_hops(parts))),
        out_shape=[
            jax.ShapeDtypeStruct((rows, width), jnp.bfloat16),
            *[jax.ShapeDtypeStruct((piece_rows, ff), jnp.bfloat16)] * len(later_hops(parts)),
        ],
        scratch_shapes=[
            pltpu.VMEM((rows, width2), jnp.bfloat16),
            pltpu.VMEM((2, width, ff), jnp.bfloat16),
            pltpu.VMEM((rows, 2 * ff), jnp.bfloat16),
            pltpu.VMEM((ff, rows), jnp.bfloat16),
            pltpu.VMEM((rows, width), jnp.bfloat16),
            pltpu.VMEM((parts, 2, piece_rows, ff), jnp.bfloat16),
            pltpu.SemaphoreType.DMA((4,)),
            pltpu.SemaphoreType.DMA((width // TERM_COLS,)),
            pltpu.SemaphoreType.DMA((parts, 2)),
        ],
        compiler_params=pltpu.CompilerParams(vmem_limit_bytes=60 << 20),
        cost_estimate=pl.CostEstimate(
            flops=8 * rows * width * ff,
            bytes_accessed=2 * (3 * rows * width + 5 * width * ff),
            transcendentals=0,
        ),
        name="rest",
    )(me, received, grads, hidden_t, w_in)
    return row_grad, dict(zip(later_hops(parts), own)), first


def rest_kernel(parts, me_ref, rows_hbm, grads_hbm, hidden_hbm, w_hbm, row_grad_hbm, *refs):
    later = later_hops(parts)
    outs, refs = refs[: len(later)], refs[len(later) :]
    rows, w, grads, hidden_t, row_grad, terms, in_sems, row_sems, out_sems = refs
    _, width, ff = w.shape
    me = me_ref[0]
    sources = [grads_hbm, w_hbm, hidden_hbm, rows_hbm]
    targets = [grads, w, hidden_t, rows]
    arrive = [
        pltpu.make_async_copy(a, b, in_sems.at[k]) for k, (a, b) in enumerate(zip(sources, targets))
    ]
    for copy in arrive:
        copy.start()
    arrive[0].wait()
    arrive[1].wait()
    leave = []
    def row_copy(i):
        cols = (slice(None), pl.ds(pl.multiple_of(i * TERM_COLS, TERM_COLS), TERM_COLS))
        return pltpu.make_async_copy(row_grad.at[cols], row_grad_hbm.at[cols], row_sems.at[i])

    @pl.loop(0, width // TERM_COLS)
    def _(i):
        span = pl.ds(pl.multiple_of(i * TERM_COLS, TERM_COLS), TERM_COLS)
        value = matmul(grads[:, :ff], w[0, span, :], ((1,), (1,)))
        value = value + matmul(grads[:, ff:], w[1, span, :], ((1,), (1,)))
        row_grad[:, span] = value.astype(jnp.bfloat16)
        row_copy(i).start()

    leave += [row_copy(i) for i in range(width // TERM_COLS)]
    arrive[2].wait()
    arrive[3].wait()
    out_copies = {
        (k, c): pltpu.make_async_copy(terms.at[k, c], out, out_sems.at[k, c])
        for (k, c), out in zip(later, outs)
    }
    whole = [k for k in range(parts) if (k, 0) in later and (k, 1) in later]
    first = parts - (parts - 1) // 2 + 1

    def fill(k, chains):
        def store(c, r, f, value):
            terms[k, c, r, f] = value

        block_terms(k, chains, me, parts, rows, grads, hidden_t, store)

    for k, c in later:
        if k not in whole:
            fill(k, [c])
            out_copies[k, c].start()

    @pl.loop(0, len(whole))
    def _(i):
        k = lax.rem(first + i, parts)
        fill(k, [0, 1])
        for j in whole:

            @pl.when(k == j)
            def _():
                out_copies[j, 0].start()
                out_copies[j, 1].start()

    leave += list(out_copies.values())
    for copy in leave:
        copy.wait()


def finish_kernel(own_a, right_a, left_a, own_b, right_b, left_b, gate_ref, up_ref, down_ref):
    half = own_a.shape[0] // 3
    block = 2 * half
    for c, (own, right, left) in enumerate(((own_a, right_a, left_a), (own_b, right_b, left_b))):
        total = (
            own[...].astype(jnp.float32)
            + right[...].astype(jnp.float32)
            + left[...].astype(jnp.float32)
        ).astype(gate_ref.dtype)
        span = slice(c * half, (c + 1) * half)
        gate_ref[0, span, :] = total[:half]
        up_ref[0, span, :] = total[half : 2 * half]
        for h in range(total.shape[1] // block):
            down_ref[0, h * block + c * half : h * block + (c + 1) * half, :] = total[
                2 * half :, h * block : (h + 1) * block
            ]


def finish(*parts):
    piece_rows, ff = parts[0].shape
    rows = 2 * piece_rows // 3
    vmem = pl.BlockSpec(memory_space=pltpu.VMEM)
    return pl.pallas_call(
        finish_kernel,
        in_specs=[vmem] * 6,
        out_specs=[vmem] * 3,
        out_shape=[
            jax.ShapeDtypeStruct((1, rows, ff), parts[0].dtype),
            jax.ShapeDtypeStruct((1, rows, ff), parts[0].dtype),
            jax.ShapeDtypeStruct((1, ff, rows), parts[0].dtype),
        ],
        compiler_params=pltpu.CompilerParams(vmem_limit_bytes=60 << 20),
        name="finish",
    )(*parts)


def shift(a, by):
    n = lax.axis_size("dp")
    return lax.ppermute(a, "dp", [(i, (i + by) % n) for i in range(n)])


def ring_gather(shard, far):
    n = lax.axis_size("dp")
    moved = {1: [shard], -1: [shard]}
    for by in (far, -far):
        for _ in range(n // 2 if by == far else (n - 1) // 2):
            moved[by].append(shift(moved[by][-1], by))
    right, left = moved[1], moved[-1]
    return [right[k] if k < len(right) else left[n - k] for k in range(n)]


def ring_scatter(own, first, n):
    half = first[0].shape[0] // 2
    arrived = {
        (c, by): a[c * half : (c + 1) * half]
        for a, by in zip(first, (1, -1))
        for c in range(2)
    }
    left = {
        (c, by): hops[c] if by > 0 else n - hops[c]
        for hops, by in zip(first_hops(n), (1, -1))
        for c in range(2)
    }
    for _ in range(n // 2):
        for group in (((0, 1), (1, -1)), ((1, 1), (0, -1))):
            going = [key for key in group if left[key] > 1]
            for c, by in going:
                left[c, by] -= 1
                mine = own[by * left[c, by] % n, c].astype(jnp.float32)
                total = arrived[c, by].astype(jnp.float32) + mine
                arrived[c, by] = shift(total.astype(jnp.bfloat16), by)
            if any(left[key] > 1 for key in going):
                met = lax.optimization_barrier([arrived[key] for key in going])
                arrived.update(zip(going, met))
    return [a for c in range(2) for a in (own[0, c], arrived[c, 1], arrived[c, -1])]


def local(tokens, cotangent, routes, gate_values, w_gate, w_up, w_down):
    experts = lax.axis_size("expert")
    tok_dev, model_width = tokens.shape
    fan_out = routes.shape[1]
    capacity = min(tok_dev, 3 * tok_dev * fan_out // (2 * experts))

    def exchange(rows):
        return lax.all_to_all(
            rows.reshape(experts, capacity, rows.shape[1]),
            "expert",
            split_axis=0,
            concat_axis=0,
            tiled=True,
        ).reshape(rows.shape)

    packed, rank, shard_a, shard_b = pack(
        routes, gate_values, tokens, cotangent, w_gate, w_up, w_down, experts, capacity
    )
    received = exchange(packed)
    pieces_a, pieces_b = ring_gather(shard_a, 1), ring_gather(shard_b, -1)
    pieces = [p for pair in zip(pieces_a, pieces_b) for p in pair]
    me = lax.axis_index("dp").astype(jnp.int32).reshape(1)
    row_grad, own, first = terms_of(me, received, pieces)
    hops = [shift(a, by) for a, by in zip(first, (1, -1))]
    hops = lax.optimization_barrier(hops)
    sums = ring_scatter(own, hops, lax.axis_size("dp"))

    returned = exchange(row_grad)
    place = rank[:, None, :] == jnp.arange(capacity, dtype=jnp.int32)[None, :, None]
    place = place.reshape(experts * capacity, tok_dev).astype(jnp.bfloat16)
    token_grad = matmul(place, returned, ((0,), (0,))).astype(jnp.bfloat16)
    token_grad, *sums = lax.optimization_barrier((token_grad, *sums))
    return (token_grad, *finish(*sums))


def solution(mesh):
    in_specs = (
        P(("expert", "dp"), None),
        P(("expert", "dp"), None),
        P(("expert", "dp"), None),
        P(("expert", "dp"), None),
        P("expert", "dp", None),
        P("expert", "dp", None),
        P("expert", None, "dp"),
    )
    out_specs = (
        P(("expert", "dp"), None),
        P("expert", "dp", None),
        P("expert", "dp", None),
        P("expert", None, "dp"),
    )
    return jax.shard_map(local, mesh=mesh, in_specs=in_specs, out_specs=out_specs, check_vma=False)
```

```python
import jax
import jax.numpy as jnp
from jax import lax
from jax.experimental import pallas as pl
from jax.experimental.pallas import tpu as pltpu
from jax.sharding import PartitionSpec as P

ROWS = 384
COLS = 256
TERM_COLS = 512
PACK_COLS = 512


def matmul(a, b, dims=((1,), (0,))):
    return lax.dot_general(a, b, (dims, ((), ())), preferred_element_type=jnp.float32)


def pack_kernel(
    capacity,
    routes_ref,
    gate_ref,
    tokens_hbm,
    cotangent_hbm,
    w_gate_hbm,
    w_up_hbm,
    w_down_hbm,
    packed_hbm,
    rank_ref,
    shard_a_hbm,
    shard_b_hbm,
    tokens,
    shards,
    down,
    place,
    packed,
    in_sems,
    w_sems,
    shard_sems,
    out_sems,
):
    experts, tok_dev = rank_ref.shape
    width = tokens_hbm.shape[1]
    sources = [tokens_hbm, cotangent_hbm]
    row_copies = [
        pltpu.make_async_copy(sources[k], tokens.at[k], in_sems.at[k]) for k in range(2)
    ]
    w_copies = [
        pltpu.make_async_copy(w_gate_hbm.at[0], shards.at[0], w_sems.at[0]),
        pltpu.make_async_copy(w_up_hbm.at[0], shards.at[1], w_sems.at[1]),
        pltpu.make_async_copy(w_down_hbm.at[0], down, w_sems.at[2]),
    ]
    for copy in row_copies + w_copies:
        copy.start()

    ids = lax.broadcasted_iota(jnp.int32, (experts, tok_dev), 0)
    gates = gate_ref[...].astype(jnp.float32)
    member = jnp.zeros((experts, tok_dev), jnp.float32)
    gate = jnp.zeros((experts, tok_dev), jnp.float32)
    for k in range(routes_ref.shape[0]):
        hit = routes_ref[k : k + 1, :] == ids
        member = jnp.where(hit, 1.0, member)
        gate = jnp.where(hit, gates[k : k + 1, :], gate)
    row = lax.broadcasted_iota(jnp.int32, (tok_dev, tok_dev), 0)
    col = lax.broadcasted_iota(jnp.int32, (tok_dev, tok_dev), 1)
    before = matmul(member.astype(jnp.bfloat16), (row < col).astype(jnp.bfloat16))
    rank = jnp.where(member > 0.5, before, -1.0)
    rank_ref[...] = rank.astype(jnp.int32)
    slots = lax.broadcasted_iota(jnp.int32, (capacity, tok_dev), 0).astype(jnp.float32)
    for e in range(0, experts, 2):
        here, gate_here = [], []
        for f in (e, e + 1):
            mask = jnp.broadcast_to(rank[f : f + 1, :], (capacity, tok_dev)) == slots
            here.append(jnp.where(mask, 1.0, 0.0))
            gate_here.append(
                jnp.where(mask, jnp.broadcast_to(gate[f : f + 1, :], (capacity, tok_dev)), 0.0)
            )
        span = slice(e * capacity, (e + 2) * capacity)
        place[0, span, :] = jnp.concatenate(here, axis=0).astype(place.dtype)
        place[1, span, :] = jnp.concatenate(gate_here, axis=0).astype(place.dtype)

    half = shards.shape[1] // 2
    shard_copies = [
        [
            pltpu.make_async_copy(
                shards.at[k, pl.ds(c * half, half), :],
                out.at[pl.ds(k * half, half), :],
                shard_sems.at[k, c],
            )
            for c, out in enumerate((shard_a_hbm, shard_b_hbm))
        ]
        for k in range(3)
    ]
    steps = width // PACK_COLS

    def out_copy(i):
        cols = (slice(None), pl.ds(i * PACK_COLS, PACK_COLS))
        return pltpu.make_async_copy(packed.at[cols], packed_hbm.at[cols], out_sems.at[i])

    for k in range(2):
        row_copies[k].wait()

        for i in range(steps):
            source = pl.ds(i * PACK_COLS, PACK_COLS)
            target = pl.ds((k * steps + i) * PACK_COLS, PACK_COLS)
            packed[:, target] = matmul(place[k], tokens[k, :, source]).astype(packed.dtype)
            out_copy(k * steps + i).start()

        if k == 0:
            for m in range(3):
                w_copies[m].wait()
                if m == 2:
                    shards[2] = down[...].T
                for copy in shard_copies[m]:
                    copy.start()
    for copy in sum(shard_copies, [out_copy(i) for i in range(2 * steps)]):
        copy.wait()


def pack(routes, gate_values, tokens, cotangent, w_gate, w_up, w_down, experts, capacity):
    tok_dev, width = tokens.shape
    slots = experts * capacity
    vmem = pl.BlockSpec(memory_space=pltpu.VMEM)
    hbm = pl.BlockSpec(memory_space=pl.ANY)
    return pl.pallas_call(
        lambda *refs: pack_kernel(capacity, *refs),
        in_specs=[vmem] * 2 + [hbm] * 5,
        out_specs=[hbm, vmem, hbm, hbm],
        out_shape=[
            jax.ShapeDtypeStruct((slots, 2 * width), tokens.dtype),
            jax.ShapeDtypeStruct((experts, tok_dev), jnp.int32),
            *[jax.ShapeDtypeStruct((3 * w_gate.shape[1] // 2, w_gate.shape[2]), w_gate.dtype)] * 2,
        ],
        scratch_shapes=[
            pltpu.VMEM((2, tok_dev, width), tokens.dtype),
            pltpu.VMEM((3, *w_gate.shape[1:]), w_gate.dtype),
            pltpu.VMEM(w_down.shape[1:], w_down.dtype),
            pltpu.VMEM((2, slots, tok_dev), jnp.bfloat16),
            pltpu.VMEM((slots, 2 * width), tokens.dtype),
            pltpu.SemaphoreType.DMA((2,)),
            pltpu.SemaphoreType.DMA((3,)),
            pltpu.SemaphoreType.DMA((3, 2)),
            pltpu.SemaphoreType.DMA((2 * width // PACK_COLS,)),
        ],
        compiler_params=pltpu.CompilerParams(vmem_limit_bytes=60 << 20),
        cost_estimate=pl.CostEstimate(
            flops=4 * slots * tok_dev * width,
            bytes_accessed=4 * slots * width,
            transcendentals=0,
        ),
        name="pack",
    )(routes.T, gate_values.T, tokens, cotangent, w_gate, w_up, w_down)


def first_hops(n):
    far, near = n // 2, (n - 1) // 2
    return (far, near), (n - near, n - far)


def later_hops(n):
    sent = {(k, c) for pair in first_hops(n) for c, k in enumerate(pair)}
    return [(k, c) for k in range(n) for c in range(2) if (k, c) not in sent]


def block_terms(k, chains, me, parts, rows, grads, hidden_t, store):
    width = rows.shape[1] // 2
    ff = hidden_t.shape[0]
    block = width // parts
    half = block // 2
    start = lax.rem(me + k, parts) * block
    if len(chains) == 2:
        x_cols = rows[:, pl.ds(pl.multiple_of(start, block), block)]
    else:
        x_cols = rows[:, pl.ds(pl.multiple_of(start + chains[0] * half, half), half)]
    s_cols = rows[:, pl.ds(pl.multiple_of(width + start, block), block)]
    both = matmul(x_cols, grads[...], ((0,), (0,))).astype(jnp.bfloat16)
    if len(chains) == 2:
        down = matmul(hidden_t[...], s_cols).astype(jnp.bfloat16)
    for i, c in enumerate(chains):
        span = slice(i * half, (i + 1) * half)
        store(c, slice(0, half), slice(0, ff), both[span, :ff])
        store(c, slice(half, 2 * half), slice(0, ff), both[span, ff:])
        for h in range(ff // block):
            feature = slice(h * block + c * half, h * block + (c + 1) * half)
            if len(chains) == 2:
                value = down[feature]
            else:
                value = matmul(hidden_t[feature, :], s_cols).astype(jnp.bfloat16)
            store(c, slice(2 * half, 3 * half), slice(h * block, (h + 1) * block), value)


def terms_kernel(parts, me_ref, rows_hbm, *refs):
    pieces, refs = refs[: 2 * parts], refs[2 * parts :]
    grads_hbm, hidden_hbm, w_hbm, refs = refs[0], refs[1], refs[2], refs[3:]
    firsts, refs = refs[:2], refs[2:]
    rows, w, grads, hidden_t, terms, row_sems, w_sems, keep_sems, out_sems = refs
    _, width, ff = w.shape
    n = rows.shape[0]
    block = width // parts
    half = block // 2
    me = me_ref[0]

    def row_copy(k, left, size):
        span = (pl.ds(k * ROWS, ROWS), pl.ds(left, size))
        return pltpu.make_async_copy(
            rows_hbm.at[span], rows.at[span], row_sems.at[k + (1 if left else 0) + (k > 0)]
        )

    def w_copy(m, k, c):
        start = pl.multiple_of(lax.rem(me + parts - k, parts) * block + c * half, half)
        return pltpu.make_async_copy(
            pieces[2 * k + c].at[pl.ds(m * half, half), :],
            w.at[m, pl.ds(start, half), :],
            w_sems.at[m, k, c],
        )

    x_copy = row_copy(0, 0, width)
    scaled_copy = row_copy(0, width, width)
    later = [row_copy(k, 0, 2 * width) for k in range(1, n // ROWS)]
    w_copies = [[w_copy(m, k, c) for k in range(parts) for c in range(2)] for m in range(3)]
    for copy in [x_copy, *w_copies[0], *w_copies[1], scaled_copy, *w_copies[2], *later]:
        copy.start()
    keep = [
        pltpu.make_async_copy(grads, grads_hbm, keep_sems.at[0]),
        pltpu.make_async_copy(hidden_t, hidden_hbm, keep_sems.at[1]),
        pltpu.make_async_copy(w.at[pl.ds(0, 2)], w_hbm, keep_sems.at[2]),
    ]

    for k in range(n // ROWS):
        span = slice(k * ROWS, (k + 1) * ROWS)
        if k == 0:
            x_copy.wait()
            for copy in w_copies[0]:
                copy.wait()
        else:
            later[k - 1].wait()
        x = rows[span, :width]
        gate_pre = matmul(x, w[0])
        sig = 1.0 / (1.0 + jnp.exp(-gate_pre))
        activated = gate_pre * sig
        slope = sig * (1.0 + gate_pre * (1.0 - sig))
        if k == 0:
            for copy in w_copies[1]:
                copy.wait()
        up_pre = matmul(x, w[1])
        hidden_t[:, span] = (activated * up_pre).astype(jnp.bfloat16).T
        if k == 0:
            scaled_copy.wait()
            for copy in w_copies[2]:
                copy.wait()
        hidden_grad = matmul(rows[span, width:], w[2])
        grads[span, :ff] = (hidden_grad * up_pre * slope).astype(jnp.bfloat16)
        grads[span, ff:] = (hidden_grad * activated).astype(jnp.bfloat16)
        if k == 0:
            keep[2].start()

    keep[0].start()
    keep[1].start()
    hops = first_hops(parts)
    wanted = {}
    for d, pair in enumerate(hops):
        for c, k in enumerate(pair):
            wanted.setdefault(k, {})[c] = d
    for k, chains in wanted.items():

        def store(c, r, f, value):
            terms[chains[c], c * 3 * half + r.start : c * 3 * half + r.stop, f] = value

        block_terms(k, sorted(chains), me, parts, rows, grads, hidden_t, store)
    out_copies = [pltpu.make_async_copy(terms.at[d], firsts[d], out_sems.at[d]) for d in range(2)]
    for copy in out_copies:
        copy.start()
    for copy in [*keep, *out_copies]:
        copy.wait()


def terms_of(me, received, pieces):
    rows, width2 = received.shape
    width = width2 // 2
    parts = len(pieces) // 2
    piece_rows, ff = pieces[0].shape
    hbm = pl.BlockSpec(memory_space=pl.ANY)
    grads, hidden_t, w_in, *first = pl.pallas_call(
        lambda *refs: terms_kernel(parts, *refs),
        in_specs=[pl.BlockSpec(memory_space=pltpu.SMEM)] + [hbm] * (1 + 2 * parts),
        out_specs=[hbm] * 5,
        out_shape=[
            jax.ShapeDtypeStruct((rows, 2 * ff), jnp.bfloat16),
            jax.ShapeDtypeStruct((ff, rows), jnp.bfloat16),
            jax.ShapeDtypeStruct((2, width, ff), jnp.bfloat16),
            *[jax.ShapeDtypeStruct((2 * piece_rows, ff), jnp.bfloat16)] * 2,
        ],
        scratch_shapes=[
            pltpu.VMEM((rows, width2), jnp.bfloat16),
            pltpu.VMEM((3, width, ff), jnp.bfloat16),
            pltpu.VMEM((rows, 2 * ff), jnp.bfloat16),
            pltpu.VMEM((ff, rows), jnp.bfloat16),
            pltpu.VMEM((2, 2 * piece_rows, ff), jnp.bfloat16),
            pltpu.SemaphoreType.DMA((1 + rows // ROWS,)),
            pltpu.SemaphoreType.DMA((3, parts, 2)),
            pltpu.SemaphoreType.DMA((3,)),
            pltpu.SemaphoreType.DMA((2,)),
        ],
        compiler_params=pltpu.CompilerParams(vmem_limit_bytes=60 << 20),
        cost_estimate=pl.CostEstimate(
            flops=8 * rows * width * ff,
            bytes_accessed=2 * (2 * rows * width + 6 * width * ff),
            transcendentals=rows * ff,
        ),
        name="terms",
    )(me, received, *pieces)
    row_grad, *own = pl.pallas_call(
        lambda *refs: rest_kernel(parts, *refs),
        in_specs=[pl.BlockSpec(memory_space=pltpu.SMEM)] + [hbm] * 4,
        out_specs=[hbm] * (1 + len(later_hops(parts))),
        out_shape=[
            jax.ShapeDtypeStruct((rows, width), jnp.bfloat16),
            *[jax.ShapeDtypeStruct((piece_rows, ff), jnp.bfloat16)] * len(later_hops(parts)),
        ],
        scratch_shapes=[
            pltpu.VMEM((rows, width2), jnp.bfloat16),
            pltpu.VMEM((2, width, ff), jnp.bfloat16),
            pltpu.VMEM((rows, 2 * ff), jnp.bfloat16),
            pltpu.VMEM((ff, rows), jnp.bfloat16),
            pltpu.VMEM((rows, width), jnp.bfloat16),
            pltpu.VMEM((parts, 2, piece_rows, ff), jnp.bfloat16),
            pltpu.SemaphoreType.DMA((4,)),
            pltpu.SemaphoreType.DMA((width // TERM_COLS,)),
            pltpu.SemaphoreType.DMA((parts, 2)),
        ],
        compiler_params=pltpu.CompilerParams(vmem_limit_bytes=60 << 20),
        cost_estimate=pl.CostEstimate(
            flops=8 * rows * width * ff,
            bytes_accessed=2 * (3 * rows * width + 5 * width * ff),
            transcendentals=0,
        ),
        name="rest",
    )(me, received, grads, hidden_t, w_in)
    return row_grad, dict(zip(later_hops(parts), own)), first


def rest_kernel(parts, me_ref, rows_hbm, grads_hbm, hidden_hbm, w_hbm, row_grad_hbm, *refs):
    later = later_hops(parts)
    outs, refs = refs[: len(later)], refs[len(later) :]
    rows, w, grads, hidden_t, row_grad, terms, in_sems, row_sems, out_sems = refs
    _, width, ff = w.shape
    me = me_ref[0]
    sources = [grads_hbm, w_hbm, hidden_hbm, rows_hbm]
    targets = [grads, w, hidden_t, rows]
    arrive = [
        pltpu.make_async_copy(a, b, in_sems.at[k]) for k, (a, b) in enumerate(zip(sources, targets))
    ]
    for copy in arrive:
        copy.start()
    arrive[0].wait()
    arrive[1].wait()
    leave = []
    def row_copy(i):
        cols = (slice(None), pl.ds(pl.multiple_of(i * TERM_COLS, TERM_COLS), TERM_COLS))
        return pltpu.make_async_copy(row_grad.at[cols], row_grad_hbm.at[cols], row_sems.at[i])

    for i in range(width // TERM_COLS):
        span = slice(i * TERM_COLS, (i + 1) * TERM_COLS)
        value = matmul(grads[:, :ff], w[0, span, :], ((1,), (1,)))
        value = value + matmul(grads[:, ff:], w[1, span, :], ((1,), (1,)))
        row_grad[:, span] = value.astype(jnp.bfloat16)
        row_copy(i).start()

    leave += [row_copy(i) for i in range(width // TERM_COLS)]
    arrive[2].wait()
    arrive[3].wait()
    out_copies = {
        (k, c): pltpu.make_async_copy(terms.at[k, c], out, out_sems.at[k, c])
        for (k, c), out in zip(later, outs)
    }
    whole = [k for k in range(parts) if (k, 0) in later and (k, 1) in later]
    first = parts - (parts - 1) // 2 + 1

    def fill(k, chains):
        def store(c, r, f, value):
            terms[k, c, r, f] = value

        block_terms(k, chains, me, parts, rows, grads, hidden_t, store)

    for k, c in later:
        if k not in whole:
            fill(k, [c])
            out_copies[k, c].start()

    @pl.loop(0, len(whole))
    def _(i):
        k = lax.rem(first + i, parts)
        fill(k, [0, 1])
        for j in whole:

            @pl.when(k == j)
            def _():
                out_copies[j, 0].start()
                out_copies[j, 1].start()

    leave += list(out_copies.values())
    for copy in leave:
        copy.wait()


def finish_kernel(own_a, right_a, left_a, own_b, right_b, left_b, gate_ref, up_ref, down_ref):
    half = own_a.shape[0] // 3
    block = 2 * half
    for c, (own, right, left) in enumerate(((own_a, right_a, left_a), (own_b, right_b, left_b))):
        total = (
            own[...].astype(jnp.float32)
            + right[...].astype(jnp.float32)
            + left[...].astype(jnp.float32)
        ).astype(gate_ref.dtype)
        span = slice(c * half, (c + 1) * half)
        gate_ref[0, span, :] = total[:half]
        up_ref[0, span, :] = total[half : 2 * half]
        for h in range(total.shape[1] // block):
            down_ref[0, h * block + c * half : h * block + (c + 1) * half, :] = total[
                2 * half :, h * block : (h + 1) * block
            ]


def finish(*parts):
    piece_rows, ff = parts[0].shape
    rows = 2 * piece_rows // 3
    vmem = pl.BlockSpec(memory_space=pltpu.VMEM)
    return pl.pallas_call(
        finish_kernel,
        in_specs=[vmem] * 6,
        out_specs=[vmem] * 3,
        out_shape=[
            jax.ShapeDtypeStruct((1, rows, ff), parts[0].dtype),
            jax.ShapeDtypeStruct((1, rows, ff), parts[0].dtype),
            jax.ShapeDtypeStruct((1, ff, rows), parts[0].dtype),
        ],
        compiler_params=pltpu.CompilerParams(vmem_limit_bytes=60 << 20),
        name="finish",
    )(*parts)


def shift(a, by):
    n = lax.axis_size("dp")
    return lax.ppermute(a, "dp", [(i, (i + by) % n) for i in range(n)])


def ring_gather(shard, far):
    n = lax.axis_size("dp")
    moved = {1: [shard], -1: [shard]}
    for by in (far, -far):
        for _ in range(n // 2 if by == far else (n - 1) // 2):
            moved[by].append(shift(moved[by][-1], by))
    right, left = moved[1], moved[-1]
    return [right[k] if k < len(right) else left[n - k] for k in range(n)]


def ring_scatter(own, first, n):
    half = first[0].shape[0] // 2
    arrived = {
        (c, by): a[c * half : (c + 1) * half]
        for a, by in zip(first, (1, -1))
        for c in range(2)
    }
    left = {
        (c, by): hops[c] if by > 0 else n - hops[c]
        for hops, by in zip(first_hops(n), (1, -1))
        for c in range(2)
    }
    for _ in range(n // 2):
        for group in (((0, 1), (1, -1)), ((1, 1), (0, -1))):
            going = [key for key in group if left[key] > 1]
            for c, by in going:
                left[c, by] -= 1
                mine = own[by * left[c, by] % n, c].astype(jnp.float32)
                total = arrived[c, by].astype(jnp.float32) + mine
                arrived[c, by] = shift(total.astype(jnp.bfloat16), by)
            if any(left[key] > 1 for key in going):
                met = lax.optimization_barrier([arrived[key] for key in going])
                arrived.update(zip(going, met))
    return [a for c in range(2) for a in (own[0, c], arrived[c, 1], arrived[c, -1])]


def local(tokens, cotangent, routes, gate_values, w_gate, w_up, w_down):
    experts = lax.axis_size("expert")
    tok_dev, model_width = tokens.shape
    fan_out = routes.shape[1]
    capacity = min(tok_dev, 3 * tok_dev * fan_out // (2 * experts))

    def exchange(rows):
        return lax.all_to_all(
            rows.reshape(experts, capacity, rows.shape[1]),
            "expert",
            split_axis=0,
            concat_axis=0,
            tiled=True,
        ).reshape(rows.shape)

    packed, rank, shard_a, shard_b = pack(
        routes, gate_values, tokens, cotangent, w_gate, w_up, w_down, experts, capacity
    )
    received = exchange(packed)
    pieces_a, pieces_b = ring_gather(shard_a, 1), ring_gather(shard_b, -1)
    pieces = [p for pair in zip(pieces_a, pieces_b) for p in pair]
    me = lax.axis_index("dp").astype(jnp.int32).reshape(1)
    row_grad, own, first = terms_of(me, received, pieces)
    hops = [shift(a, by) for a, by in zip(first, (1, -1))]
    hops = lax.optimization_barrier(hops)
    sums = ring_scatter(own, hops, lax.axis_size("dp"))

    returned = exchange(row_grad)
    place = rank[:, None, :] == jnp.arange(capacity, dtype=jnp.int32)[None, :, None]
    place = place.reshape(experts * capacity, tok_dev).astype(jnp.bfloat16)
    token_grad = matmul(place, returned, ((0,), (0,))).astype(jnp.bfloat16)
    token_grad, *sums = lax.optimization_barrier((token_grad, *sums))
    return (token_grad, *finish(*sums))


def solution(mesh):
    in_specs = (
        P(("expert", "dp"), None),
        P(("expert", "dp"), None),
        P(("expert", "dp"), None),
        P(("expert", "dp"), None),
        P("expert", "dp", None),
        P("expert", "dp", None),
        P("expert", None, "dp"),
    )
    out_specs = (
        P(("expert", "dp"), None),
        P("expert", "dp", None),
        P("expert", "dp", None),
        P("expert", None, "dp"),
    )
    return jax.shard_map(local, mesh=mesh, in_specs=in_specs, out_specs=out_specs, check_vma=False)
```
